32 devices in a mesh: gz: 8 (over z, y), xy: 4 (over x, core).
Axes of the slice: x: 2, y: 2, z: 4, core: 2. Of those that a mesh axis runs over, the one named last changes fastest.
Arguments:
- up_source: bfloat16 [8, 2, 32, 1024], P('gz', None, None, 'xy'), may hold values from -6 to 6
- down_source: bfloat16 [8, 2, 32, 1024], P('gz', None, None, 'xy'), may hold values from -6 to 6
- source_layer: int32 [32], replicated, may hold values from 0 to 7, as said below
- u_factor: bfloat16 [8, 4, 4, 2, 128, 256], P('gz', 'xy'), may hold values from -0.15625 to 0.15625
- v_factor: bfloat16 [8, 4, 4, 2, 128, 256], P('gz', 'xy'), may hold values from -0.25 to 0.25
- block_rank: int32 [8, 4, 4], P('gz', 'xy'), may hold values from 1 to 4
Outputs:
- up_trace: bfloat16 [8, 2, 32, 1024], P('gz', None, None, 'xy')
- down_trace: bfloat16 [8, 2, 32, 1024], P('gz', None, None, 'xy')
The draws below stay inside these ranges and needn't reach their ends.
Inputs may be any that keep to these rules, and one draw needn't show every extreme that they name: `source_layer`: the index of the layer slab in which source s lies; source 0 lies in slab 0 and source 1 in slab 8 - 1. `block_rank`: block (i, j) of interface l has rank 32 times this number.
All inputs are finite; a program needn't handle non-finite values.
Results may differ from the reference program's by a relative error of at most 0.007.
Values may be sent and summed in bfloat16 or wider, within the bound.
A program may use at most 64 MiB of HBM per device.

```python
import jax
import jax.numpy as jnp
from jax import lax

BLK = 256
RMAX = 128
SRC = 32
STEPS = 3
LAYERS = 8
N = 1024
NB = 4
RANK_STEP = 32


def draw_source_layer(key, part):
    drawn = jax.random.randint(key, (SRC,), 0, LAYERS, dtype=jnp.int32)
    position = jnp.arange(SRC, dtype=jnp.int32)
    drawn = jnp.where(position == 0, jnp.zeros_like(drawn), drawn)
    drawn = jnp.where(position == 1, jnp.full_like(drawn, LAYERS - 1), drawn)
    return drawn


def set_ends(result, stream_key, least, largest):
    longest = result.shape.index(max(result.shape))
    spots = []
    for shift in (0, 1):
        where = [jax.random.randint(jax.random.fold_in(stream_key, axis), (), 0, length) for axis, length in enumerate(result.shape)]
        where[longest] = (where[longest] + shift) % result.shape[longest]
        spots.append(tuple(where))
    return result.at[spots[0]].set(least).at[spots[1]].set(largest)


def shard_levels(own_key, shape, split, low, high):
    def one(dim, parts):
        draws = jax.random.uniform(jax.random.fold_in(jax.random.fold_in(own_key, 6), dim), (parts,), jnp.float32, low / len(split), high / len(split))
        return jnp.repeat(jnp.exp(draws), shape[dim] // parts).reshape((-1,) + (1,) * (len(shape) - dim - 1))

    level = one(*split[0])
    for cut in split[1:]:
        level = level * one(*cut)
    return level


def bell_draw(rng, dims, spread, most, shards=(), held_as=jnp.bfloat16):
    level = shard_levels(rng, dims, shards, -0.22, 0.18) if shards else 1.0
    entries = jax.random.normal(rng, dims, jnp.float32) * spread * level
    return jnp.minimum(jnp.maximum(entries, -most), most).astype(held_as)


def setup_inputs(seed: int = 0) -> dict:
    key_of = jax.random.split(jax.random.key(seed), 7)
    up_source = bell_draw(key_of[0], (LAYERS, 2, SRC, N), 1.0, 6.0, ((0, 8), (3, 4)))
    down_source = bell_draw(key_of[1], (LAYERS, 2, SRC, N), 1.0, 6.0, ((0, 8), (3, 4)))
    source_layer = draw_source_layer(jax.random.fold_in(key_of[6], 71), 0)
    u_factor = bell_draw(key_of[3], (LAYERS, NB, NB, 2, RMAX, BLK), (3 * NB * RMAX) ** -0.5, 0.15625, ((0, 8), (1, 4)))
    v_factor = bell_draw(key_of[4], (LAYERS, NB, NB, 2, RMAX, BLK), (2 * BLK) ** -0.5, 0.25, ((0, 8), (1, 4)))
    block_rank = set_ends(jax.random.randint(key_of[5], (LAYERS, NB, NB), 1, 5), jax.random.fold_in(key_of[5], 1), 1, 4).astype(jnp.int32)
    return dict(up_source=up_source, down_source=down_source, source_layer=source_layer, u_factor=u_factor, v_factor=v_factor, block_rank=block_rank)


def complex_parts(product):
    real = product[..., 0, :, 0, :] - product[..., 1, :, 1, :]
    imag = product[..., 0, :, 1, :] + product[..., 1, :, 0, :]
    return jnp.stack([real, imag], axis=-3)


def round_half(values):
    return lax.optimization_barrier(values.astype(jnp.bfloat16)).astype(jnp.float32)


def layer_apply(u_layer, v_layer, rank_layer, up_layer, above_layer):
    keep_rank = jnp.arange(RMAX, dtype=jnp.int32)[None, None, :] < RANK_STEP * rank_layer[:, :, None]
    u_float = u_layer.astype(jnp.float32)
    v_float = v_layer.astype(jnp.float32)
    pieces = up_layer.astype(jnp.float32).reshape(2, SRC, NB, BLK)
    up_coef = complex_parts(jnp.einsum('asjb,ijcrb->ijascr', pieces, v_float))
    up_coef = round_half(jnp.where(keep_rank[:, :, None, None, :], up_coef, 0.0))
    forward = complex_parts(jnp.einsum('ijasr,ijcrb->iascb', up_coef, u_float))
    forward = jnp.transpose(forward, (1, 2, 0, 3)).reshape(2, SRC, N)
    upper = above_layer.astype(jnp.float32).reshape(2, SRC, NB, BLK)
    down_coef = complex_parts(jnp.einsum('asib,ijcrb->ijascr', upper, u_float))
    down_coef = round_half(jnp.where(keep_rank[:, :, None, None, :], down_coef, 0.0))
    backward = complex_parts(jnp.einsum('ijasr,ijcrb->jascb', down_coef, v_float))
    backward = jnp.transpose(backward, (1, 2, 0, 3)).reshape(2, SRC, N)
    return forward, backward


def reference(up_source, down_source, source_layer, u_factor, v_factor, block_rank):
    layer_ids = jnp.arange(LAYERS, dtype=jnp.int32)
    up_mask = (layer_ids[:, None] >= source_layer[None, :])[:, None, :, None]
    down_mask = (layer_ids[:, None] <= source_layer[None, :])[:, None, :, None]
    active_up = jnp.where(up_mask, up_source, jnp.zeros_like(up_source))
    active_down = jnp.where(down_mask, down_source, jnp.zeros_like(down_source))
    up_trace = active_up
    down_trace = active_down
    for sweep_index in range(STEPS):
        upper = jnp.concatenate([down_trace[1:], jnp.zeros_like(down_trace[:1])], axis=0)
        forward, backward = lax.map(lambda items: layer_apply(*items), (u_factor, v_factor, block_rank, up_trace, upper))
        lower = jnp.concatenate([jnp.zeros_like(forward[:1]), forward[:-1]], axis=0)
        up_trace = (active_up.astype(jnp.float32) + lower).astype(jnp.bfloat16)
        down_trace = (active_down.astype(jnp.float32) + backward).astype(jnp.bfloat16)
    return up_trace, down_trace
```

```python
import functools

import jax
import jax.numpy as jnp
from jax import lax
from jax.experimental import pallas as pl
from jax.experimental.pallas import tpu as pltpu
from jax.sharding import PartitionSpec as P

STEPS = 3
MESH = pl.DeviceIdType.MESH


def kernel(
    layers, n, up_ref, down_ref, layer_ref, u_hbm, v_hbm, rank_ref, up_out, down_out,
    u_mem, v_mem, up_all, up_send, up_next, up_last, own_down, down_first, part, part_send,
    load_sem, up_ssem, up_rsem, next_ssem, next_rsem, last_ssem, last_rsem,
    first_ssem, first_rsem, part_ssem, part_rsem,
):
    layer = lax.axis_index("gz")
    me = lax.axis_index("xy")
    has_above = layer < layers - 1
    has_below = layer > 0
    rows, width = up_send.shape[1:]
    sources = rows // 2
    max_rank = u_mem.shape[2]
    others = [lax.rem(me + k, n) for k in range(n)]

    def remote(src, dst, ssem, rsem, to_layer, to_block):
        return pltpu.make_async_remote_copy(
            src_ref=src, dst_ref=dst, send_sem=ssem, recv_sem=rsem,
            device_id={"gz": to_layer, "xy": to_block}, device_id_type=MESH,
        )

    load_u = pltpu.make_async_copy(u_hbm.at[0, 0], u_mem, load_sem.at[0])
    load_v = pltpu.make_async_copy(v_hbm.at[0, 0], v_mem, load_sem.at[1])
    load_v.start()
    load_u.start()

    barrier = pltpu.get_barrier_semaphore()

    def greet(to_layer, to_block):
        pl.semaphore_signal(
            barrier, inc=1, device_id={"gz": to_layer, "xy": to_block}, device_id_type=MESH
        )

    for k in range(1, n):
        greet(layer, others[k])

    @pl.when(has_above)
    def _():
        for k in range(n):
            greet(layer + 1, others[k])

    @pl.when(has_below)
    def _():
        for k in range(n):
            greet(layer - 1, others[k])

    square = (sources, sources)
    diagonal = lax.broadcasted_iota(jnp.int32, square, 0) == lax.broadcasted_iota(jnp.int32, square, 1)
    source_layer = jnp.sum(
        jnp.where(diagonal, jnp.broadcast_to(layer_ref[...], square), 0), axis=1, keepdims=True
    )
    source_layer = jnp.broadcast_to(jnp.concatenate([source_layer, source_layer], axis=0), (rows, width))
    up_own = jnp.where(
        layer >= source_layer, up_ref[0].reshape(rows, width).astype(jnp.float32), 0.0
    ).astype(jnp.bfloat16)
    down_own = jnp.where(
        layer <= source_layer, down_ref[0].reshape(rows, width).astype(jnp.float32), 0.0
    ).astype(jnp.bfloat16)
    up_all[0, me] = up_own
    own_down[...] = down_own

    @pl.when(jnp.logical_not(has_above))
    def _():
        up_next[...] = jnp.zeros_like(up_next)
        down_first[...] = jnp.zeros_like(down_first)
        part[0] = jnp.zeros_like(part[0])
        part[1] = jnp.zeros_like(part[1])

    peers = n - 1 + jnp.where(has_above, n, 0) + jnp.where(has_below, n, 0)
    pl.semaphore_wait(barrier, peers)

    def gather(k):
        return remote(
            up_all.at[0, me], up_all.at[0, me], up_ssem.at[0, k], up_rsem.at[0, me], layer, others[k]
        )

    def next_up():
        return remote(up_all.at[0, me], up_next, next_ssem, next_rsem, layer - 1, me)

    def first_down():
        return remote(own_down, down_first, first_ssem, first_rsem, layer - 1, me)

    def up_step(t, k):
        return remote(
            up_send.at[t], up_all.at[t + 1, me], up_ssem.at[t + 1, k], up_rsem.at[t + 1, me],
            layer + 1, others[k],
        )

    def last_up():
        return remote(up_send.at[STEPS - 1], up_last, last_ssem, last_rsem, layer + 1, me)

    def part_step(t, k):
        to_layer = layer if t == STEPS - 1 else layer - 1
        return remote(
            part_send.at[t, k], part.at[t, me], part_ssem.at[t, k], part_rsem.at[t, me],
            to_layer, others[k],
        )

    def arrived(ref, rsem):
        remote(ref, ref, next_ssem, rsem, layer, me).wait_recv()

    for k in range(1, n):
        gather(k).start()

    @pl.when(has_below)
    def _():
        first_down().start()
        next_up().start()

    rank_index = lax.broadcasted_iota(jnp.int32, (sources, max_rank), 1)

    def coefficients(trace, factor, block):
        product = lax.dot_general(
            trace, factor.reshape(2 * max_rank, width), (((1,), (1,)), ((), ())),
            preferred_element_type=jnp.float32,
        )
        keep = rank_index < (max_rank // 4) * rank_ref[0, 0, block]
        real = product[:sources, :max_rank] - product[sources:, max_rank:]
        imag = product[:sources, max_rank:] + product[sources:, :max_rank]
        real = jnp.where(keep, real, 0.0)
        imag = jnp.where(keep, imag, 0.0)
        return jnp.concatenate(
            [jnp.concatenate([real, -imag], axis=1), jnp.concatenate([imag, real], axis=1)], axis=0
        ).astype(jnp.bfloat16)

    def expand(coef, factor):
        return jnp.dot(
            coef, factor.reshape(2 * max_rank, width), preferred_element_type=jnp.float32
        )

    load_v.wait()
    load_u.wait()

    for t in range(STEPS):
        held = 0 if t == 0 else jnp.where(has_below, t, 0)
        if t > 0:

            @pl.when(has_below)
            def _():
                for k in range(n):
                    arrived(up_all.at[t, others[k]], up_rsem.at[t, others[k]])

        else:
            for k in range(1, n):
                arrived(up_all.at[0, others[k]], up_rsem.at[0, others[k]])

            @pl.when(has_above)
            def _():
                arrived(up_next, next_rsem)

        total = up_next[...].astype(jnp.float32)
        for k in range(n):
            block = others[k]
            coef = coefficients(up_all[held, block], v_mem[block], block)
            total = total + expand(coef, u_mem[block])
        up_send[t] = total.astype(jnp.bfloat16)

        @pl.when(has_above)
        def _():
            if t < STEPS - 1:
                for k in range(n):
                    up_step(t, k).start()
            else:
                last_up().start()

        @pl.when(has_above)
        def _():
            if t == 0:
                arrived(down_first, first_rsem)
            else:
                for k in range(n):
                    arrived(part.at[t - 1, others[k]], part_rsem.at[t - 1, others[k]])

        down = down_first[...]
        if t > 0:
            total = down.astype(jnp.float32)
            for k in range(n):
                total = total + part[t - 1, others[k]].astype(jnp.float32)
            down = total.astype(jnp.bfloat16)
        last = t == STEPS - 1
        own_part = None
        for k in [*range(1, n), 0]:
            block = others[k]
            piece = expand(coefficients(down, u_mem[block], block), v_mem[block])
            if last and k == 0:
                own_part = piece
            else:
                part_send[t, k] = piece.astype(jnp.bfloat16)
        if last:
            for k in range(1, n):
                part_step(t, k).start()
        else:

            @pl.when(has_below)
            def _():
                for k in [*range(1, n), 0]:
                    part_step(t, k).start()

    total = own_down[...].astype(jnp.float32) + own_part
    for k in range(1, n):
        arrived(part.at[STEPS - 1, others[k]], part_rsem.at[STEPS - 1, others[k]])
        total = total + part[STEPS - 1, others[k]].astype(jnp.float32)
    down_out[0] = total.astype(jnp.bfloat16).reshape(2, sources, width)

    @pl.when(has_below)
    def _():
        arrived(up_last, last_rsem)
        up_out[0] = up_last[...].reshape(2, sources, width)

    @pl.when(jnp.logical_not(has_below))
    def _():
        up_out[0] = up_all[0, me].reshape(2, sources, width)

    for k in range(1, n):
        gather(k).wait_send()
        part_step(STEPS - 1, k).wait_send()

    @pl.when(has_below)
    def _():
        first_down().wait_send()
        next_up().wait_send()
        for t in range(STEPS - 1):
            for k in range(n):
                part_step(t, k).wait_send()

    @pl.when(has_above)
    def _():
        for t in range(STEPS - 1):
            for k in range(n):
                up_step(t, k).wait_send()
        last_up().wait_send()


def solution(mesh):
    layers, n = mesh.shape["gz"], mesh.shape["xy"]

    def on_device(up_source, down_source, source_layer, u_factor, v_factor, block_rank):
        _, _, sources, width = up_source.shape
        rows = 2 * sources
        trace = (rows, width)
        vmem = pl.BlockSpec(memory_space=pltpu.VMEM)
        smem = pl.BlockSpec(memory_space=pltpu.SMEM)
        anywhere = pl.BlockSpec(memory_space=pl.ANY)
        dma = pltpu.SemaphoreType.DMA
        return pl.pallas_call(
            functools.partial(kernel, layers, n),
            out_shape=(
                jax.ShapeDtypeStruct(up_source.shape, jnp.bfloat16),
                jax.ShapeDtypeStruct(down_source.shape, jnp.bfloat16),
            ),
            in_specs=[vmem, vmem, vmem, anywhere, anywhere, smem],
            out_specs=(vmem, vmem),
            scratch_shapes=[
                pltpu.VMEM(u_factor.shape[2:], jnp.bfloat16),
                pltpu.VMEM(v_factor.shape[2:], jnp.bfloat16),
                pltpu.VMEM((STEPS, n, *trace), jnp.bfloat16),
                pltpu.VMEM((STEPS, *trace), jnp.bfloat16),
                pltpu.VMEM(trace, jnp.bfloat16),
                pltpu.VMEM(trace, jnp.bfloat16),
                pltpu.VMEM(trace, jnp.bfloat16),
                pltpu.VMEM(trace, jnp.bfloat16),
                pltpu.VMEM((STEPS, n, *trace), jnp.bfloat16),
                pltpu.VMEM((STEPS, n, *trace), jnp.bfloat16),
                dma((2,)),
                dma((STEPS, n)),
                dma((STEPS, n)),
                dma,
                dma,
                dma,
                dma,
                dma,
                dma,
                dma((STEPS, n)),
                dma((STEPS, n)),
            ],
            compiler_params=pltpu.CompilerParams(collective_id=0, has_side_effects=True),
        )(up_source, down_source, source_layer.reshape(1, sources), u_factor, v_factor, block_rank)

    in_specs = (
        P("gz", None, None, "xy"),
        P("gz", None, None, "xy"),
        P(),
        P("gz", "xy", None, None, None, None),
        P("gz", "xy", None, None, None, None),
        P("gz", "xy", None),
    )
    out_specs = (P("gz", None, None, "xy"), P("gz", None, None, "xy"))
    return jax.shard_map(
        on_device, mesh=mesh, in_specs=in_specs, out_specs=out_specs, check_vma=False
    )
```

```python
import functools

import jax
import jax.numpy as jnp
from jax import lax
from jax.experimental import pallas as pl
from jax.experimental.pallas import tpu as pltpu
from jax.sharding import PartitionSpec as P

STEPS = 3
MESH = pl.DeviceIdType.MESH


def kernel(
    layers, n, up_ref, down_ref, layer_ref, u_hbm, v_hbm, rank_ref, up_out, down_out,
    u_mem, v_mem, up_all, up_send, up_next, up_last, own_down, down_first, part, part_send,
    twin_part, twin_send, last_in, last_send,
    load_sem, up_ssem, up_rsem, next_ssem, next_rsem, last_ssem, last_rsem,
    first_ssem, first_rsem, part_ssem, part_rsem,
    relay_ssem, twin_ssem, twin_rsem, last_part_ssem, last_part_rsem,
):
    layer = lax.axis_index("gz")
    me = lax.axis_index("xy")
    has_above = layer < layers - 1
    has_below = layer > 0
    rows, width = up_send.shape[1:]
    sources = rows // 2
    max_rank = u_mem.shape[2]
    others = [lax.rem(me + k, n) for k in range(n)]
    core = lax.rem(me, 2)
    twin = me + 1 - 2 * core
    like = [lax.rem(me + 2 * k, n) for k in range(n // 2)]
    unlike = [lax.rem(twin + 2 * k, n) for k in range(n // 2)]
    chip = me // 2

    def remote(src, dst, ssem, rsem, to_layer, to_block):
        return pltpu.make_async_remote_copy(
            src_ref=src, dst_ref=dst, send_sem=ssem, recv_sem=rsem,
            device_id={"gz": to_layer, "xy": to_block}, device_id_type=MESH,
        )

    load_u = pltpu.make_async_copy(u_hbm.at[0, 0], u_mem, load_sem.at[0])
    load_v = pltpu.make_async_copy(v_hbm.at[0, 0], v_mem, load_sem.at[1])
    load_v.start()
    load_u.start()

    barrier = pltpu.get_barrier_semaphore()

    def greet(to_layer, to_block):
        pl.semaphore_signal(
            barrier, inc=1, device_id={"gz": to_layer, "xy": to_block}, device_id_type=MESH
        )

    for k in range(1, n):
        greet(layer, others[k])

    @pl.when(has_above)
    def _():
        for k in range(n // 2):
            greet(layer + 1, like[k])

    @pl.when(has_below)
    def _():
        for k in range(n // 2):
            greet(layer - 1, like[k])

    square = (sources, sources)
    diagonal = lax.broadcasted_iota(jnp.int32, square, 0) == lax.broadcasted_iota(jnp.int32, square, 1)
    source_layer = jnp.sum(
        jnp.where(diagonal, jnp.broadcast_to(layer_ref[...], square), 0), axis=1, keepdims=True
    )
    source_layer = jnp.broadcast_to(jnp.concatenate([source_layer, source_layer], axis=0), (rows, width))
    up_own = jnp.where(
        layer >= source_layer, up_ref[0].reshape(rows, width).astype(jnp.float32), 0.0
    ).astype(jnp.bfloat16)
    down_own = jnp.where(
        layer <= source_layer, down_ref[0].reshape(rows, width).astype(jnp.float32), 0.0
    ).astype(jnp.bfloat16)
    up_all[0, me] = up_own
    own_down[...] = down_own

    @pl.when(jnp.logical_not(has_above))
    def _():
        up_next[...] = jnp.zeros_like(up_next)
        down_first[...] = jnp.zeros_like(down_first)
        part[0] = jnp.zeros_like(part[0])
        part[1] = jnp.zeros_like(part[1])

    peers = n - 1 + jnp.where(has_above, n // 2, 0) + jnp.where(has_below, n // 2, 0)
    pl.semaphore_wait(barrier, peers)

    def gather(k):
        return remote(
            up_all.at[0, me], up_all.at[0, me], up_ssem.at[0, k], up_rsem.at[0, me], layer, others[k]
        )

    def next_up():
        return remote(up_all.at[0, me], up_next, next_ssem, next_rsem, layer - 1, me)

    def first_down():
        return remote(own_down, down_first, first_ssem, first_rsem, layer - 1, me)

    def up_step(t, k):
        return remote(
            up_send.at[t], up_all.at[t + 1, me], up_ssem.at[t + 1, k], up_rsem.at[t + 1, me],
            layer + 1, like[k],
        )

    def relay(t, k):
        slot = up_all.at[t, like[k]]
        return remote(slot, slot, relay_ssem.at[t - 1, k], up_rsem.at[t, like[k]], layer, twin)

    def last_up():
        return remote(up_send.at[STEPS - 1], up_last, last_ssem, last_rsem, layer + 1, me)

    def part_step(t, k):
        return remote(
            part_send.at[t, k], part.at[t, chip], part_ssem.at[t, k], part_rsem.at[t, chip],
            layer - 1, like[k],
        )

    def twin_step(t, k):
        place = unlike[k] // 2
        return remote(
            twin_send.at[t, k], twin_part.at[t, place], twin_ssem.at[t, k], twin_rsem.at[t, place],
            layer, twin,
        )

    def last_part(k):
        return remote(
            last_send.at[k], last_in.at[me], last_part_ssem.at[k], last_part_rsem.at[me],
            layer, others[k],
        )

    def arrived(ref, rsem):
        remote(ref, ref, next_ssem, rsem, layer, me).wait_recv()

    for k in range(1, n):
        gather(k).start()

    @pl.when(has_below)
    def _():
        first_down().start()
        next_up().start()

    rank_index = lax.broadcasted_iota(jnp.int32, (sources, max_rank), 1)

    def coefficients(trace, factor, block):
        product = lax.dot_general(
            trace, factor.reshape(2 * max_rank, width), (((1,), (1,)), ((), ())),
            preferred_element_type=jnp.float32,
        )
        keep = rank_index < (max_rank // 4) * rank_ref[0, 0, block]
        real = product[:sources, :max_rank] - product[sources:, max_rank:]
        imag = product[:sources, max_rank:] + product[sources:, :max_rank]
        real = jnp.where(keep, real, 0.0)
        imag = jnp.where(keep, imag, 0.0)
        return jnp.concatenate(
            [jnp.concatenate([real, -imag], axis=1), jnp.concatenate([imag, real], axis=1)], axis=0
        ).astype(jnp.bfloat16)

    def expand(coef, factor):
        return jnp.dot(
            coef, factor.reshape(2 * max_rank, width), preferred_element_type=jnp.float32
        )

    load_v.wait()
    load_u.wait()

    for t in range(STEPS):
        held = 0 if t == 0 else jnp.where(has_below, t, 0)
        if t > 0:

            @pl.when(has_below)
            def _():
                for k in range(n // 2):
                    arrived(up_all.at[t, like[k]], up_rsem.at[t, like[k]])
                    relay(t, k).start()
                for k in range(n // 2):
                    arrived(up_all.at[t, unlike[k]], up_rsem.at[t, unlike[k]])

        else:
            for k in range(1, n):
                arrived(up_all.at[0, others[k]], up_rsem.at[0, others[k]])

            @pl.when(has_above)
            def _():
                arrived(up_next, next_rsem)

        total = up_next[...].astype(jnp.float32)
        for k in range(n):
            block = others[k]
            coef = coefficients(up_all[held, block], v_mem[block], block)
            total = total + expand(coef, u_mem[block])
        up_send[t] = total.astype(jnp.bfloat16)

        @pl.when(has_above)
        def _():
            if t < STEPS - 1:
                for k in reversed(range(n // 2)):
                    up_step(t, k).start()
            else:
                last_up().start()

        @pl.when(has_above)
        def _():
            if t == 0:
                arrived(down_first, first_rsem)
            else:
                for k in range(n // 2):
                    place = like[k] // 2
                    arrived(part.at[t - 1, place], part_rsem.at[t - 1, place])

        down = down_first[...]
        if t > 0:
            total = down.astype(jnp.float32)
            for k in range(n // 2):
                total = total + part[t - 1, like[k] // 2].astype(jnp.float32)
            down = total.astype(jnp.bfloat16)

        def piece(block):
            return expand(coefficients(down, u_mem[block], block), v_mem[block])

        if t < STEPS - 1:
            for k in range(n // 2):
                twin_send[t, k] = piece(unlike[k]).astype(jnp.bfloat16)
                twin_step(t, k).start()
            pieces = [piece(like[k]) for k in range(n // 2)]
            for k in range(n // 2):
                place = like[k] // 2
                arrived(twin_part.at[t, place], twin_rsem.at[t, place])
                part_send[t, k] = (pieces[k] + twin_part[t, place].astype(jnp.float32)).astype(
                    jnp.bfloat16
                )

            @pl.when(has_below)
            def _():
                for k in reversed(range(n // 2)):
                    part_step(t, k).start()

        else:
            for k in range(1, n):
                last_send[k] = piece(others[k]).astype(jnp.bfloat16)
                last_part(k).start()
            own_part = piece(me)

    total = own_down[...].astype(jnp.float32) + own_part
    for k in range(1, n):
        arrived(last_in.at[others[k]], last_part_rsem.at[others[k]])
        total = total + last_in[others[k]].astype(jnp.float32)
    down_out[0] = total.astype(jnp.bfloat16).reshape(2, sources, width)

    @pl.when(has_below)
    def _():
        arrived(up_last, last_rsem)
        up_out[0] = up_last[...].reshape(2, sources, width)

    @pl.when(jnp.logical_not(has_below))
    def _():
        up_out[0] = up_all[0, me].reshape(2, sources, width)

    for k in range(1, n):
        gather(k).wait_send()
        last_part(k).wait_send()
    for t in range(STEPS - 1):
        for k in range(n // 2):
            twin_step(t, k).wait_send()

    @pl.when(has_below)
    def _():
        first_down().wait_send()
        next_up().wait_send()
        for t in range(STEPS - 1):
            for k in range(n // 2):
                part_step(t, k).wait_send()
                relay(t + 1, k).wait_send()

    @pl.when(has_above)
    def _():
        for t in range(STEPS - 1):
            for k in range(n // 2):
                up_step(t, k).wait_send()
        last_up().wait_send()


def solution(mesh):
    layers, n = mesh.shape["gz"], mesh.shape["xy"]

    def on_device(up_source, down_source, source_layer, u_factor, v_factor, block_rank):
        _, _, sources, width = up_source.shape
        rows = 2 * sources
        trace = (rows, width)
        vmem = pl.BlockSpec(memory_space=pltpu.VMEM)
        smem = pl.BlockSpec(memory_space=pltpu.SMEM)
        anywhere = pl.BlockSpec(memory_space=pl.ANY)
        dma = pltpu.SemaphoreType.DMA
        return pl.pallas_call(
            functools.partial(kernel, layers, n),
            out_shape=(
                jax.ShapeDtypeStruct(up_source.shape, jnp.bfloat16),
                jax.ShapeDtypeStruct(down_source.shape, jnp.bfloat16),
            ),
            in_specs=[vmem, vmem, vmem, anywhere, anywhere, smem],
            out_specs=(vmem, vmem),
            scratch_shapes=[
                pltpu.VMEM(u_factor.shape[2:], jnp.bfloat16),
                pltpu.VMEM(v_factor.shape[2:], jnp.bfloat16),
                pltpu.VMEM((STEPS, n, *trace), jnp.bfloat16),
                pltpu.VMEM((STEPS, *trace), jnp.bfloat16),
                pltpu.VMEM(trace, jnp.bfloat16),
                pltpu.VMEM(trace, jnp.bfloat16),
                pltpu.VMEM(trace, jnp.bfloat16),
                pltpu.VMEM(trace, jnp.bfloat16),
                pltpu.VMEM((STEPS - 1, n // 2, *trace), jnp.bfloat16),
                pltpu.VMEM((STEPS - 1, n // 2, *trace), jnp.bfloat16),
                pltpu.VMEM((STEPS - 1, n // 2, *trace), jnp.bfloat16),
                pltpu.VMEM((STEPS - 1, n // 2, *trace), jnp.bfloat16),
                pltpu.VMEM((n, *trace), jnp.bfloat16),
                pltpu.VMEM((n, *trace), jnp.bfloat16),
                dma((2,)),
                dma((STEPS, n)),
                dma((STEPS, n)),
                dma,
                dma,
                dma,
                dma,
                dma,
                dma,
                dma((STEPS - 1, n // 2)),
                dma((STEPS - 1, n // 2)),
                dma((STEPS - 1, n // 2)),
                dma((STEPS - 1, n // 2)),
                dma((STEPS - 1, n // 2)),
                dma((n,)),
                dma((n,)),
            ],
            compiler_params=pltpu.CompilerParams(collective_id=0, has_side_effects=True),
        )(up_source, down_source, source_layer.reshape(1, sources), u_factor, v_factor, block_rank)

    in_specs = (
        P("gz", None, None, "xy"),
        P("gz", None, None, "xy"),
        P(),
        P("gz", "xy", None, None, None, None),
        P("gz", "xy", None, None, None, None),
        P("gz", "xy", None),
    )
    out_specs = (P("gz", None, None, "xy"), P("gz", None, None, "xy"))
    return jax.shard_map(
        on_device, mesh=mesh, in_specs=in_specs, out_specs=out_specs, check_vma=False
    )
```

```python
import functools

import jax
import jax.numpy as jnp
from jax import lax
from jax.experimental import pallas as pl
from jax.experimental.pallas import tpu as pltpu
from jax.sharding import PartitionSpec as P

STEPS = 3
MESH = pl.DeviceIdType.MESH


def kernel(
    layers, n, up_hbm, down_hbm, layer_hbm, u_hbm, v_hbm, rank_hbm, up_out, down_out,
    up_ref, down_ref, layer_ref, rank_ref, down_done,
    u_mem, v_mem, up_all, up_send, up_next, up_last, own_down, down_first, part, part_send,
    twin_part, twin_send, last_in, last_send,
    load_sem, up_ssem, up_rsem, next_ssem, next_rsem, last_ssem, last_rsem,
    first_ssem, first_rsem, part_ssem, part_rsem,
    relay_ssem, twin_ssem, twin_rsem, last_part_ssem, last_part_rsem,
):
    layer = lax.axis_index("gz")
    me = lax.axis_index("xy")
    has_above = layer < layers - 1
    has_below = layer > 0
    rows, width = up_send.shape[1:]
    sources = rows // 2
    max_rank = u_mem.shape[2]
    others = [lax.rem(me + k, n) for k in range(n)]
    core = lax.rem(me, 2)
    twin = me + 1 - 2 * core
    like = [lax.rem(me + 2 * k, n) for k in range(n // 2)]
    unlike = [lax.rem(twin + 2 * k, n) for k in range(n // 2)]
    chip = me // 2

    def remote(src, dst, ssem, rsem, to_layer, to_block):
        return pltpu.make_async_remote_copy(
            src_ref=src, dst_ref=dst, send_sem=ssem, recv_sem=rsem,
            device_id={"gz": to_layer, "xy": to_block}, device_id_type=MESH,
        )

    load_u = pltpu.make_async_copy(u_hbm.at[0, 0], u_mem, load_sem.at[0])
    load_v = pltpu.make_async_copy(v_hbm.at[0, 0], v_mem, load_sem.at[1])
    small = [
        pltpu.make_async_copy(src, dst, load_sem.at[2 + i])
        for i, (src, dst) in enumerate(
            [(layer_hbm, layer_ref), (up_hbm.at[0], up_ref), (down_hbm.at[0], down_ref), (rank_hbm, rank_ref)]
        )
    ]
    for load in small:
        load.start()

    barrier = pltpu.get_barrier_semaphore()

    def greet(to_layer, to_block):
        pl.semaphore_signal(
            barrier, inc=1, device_id={"gz": to_layer, "xy": to_block}, device_id_type=MESH
        )

    for k in range(1, n):
        greet(layer, others[k])

    @pl.when(has_above)
    def _():
        for k in range(n // 2):
            greet(layer + 1, like[k])

    @pl.when(has_below)
    def _():
        for k in range(n // 2):
            greet(layer - 1, like[k])

    load_v.start()
    load_u.start()
    for load in small:
        load.wait()
    square = (sources, sources)
    diagonal = lax.broadcasted_iota(jnp.int32, square, 0) == lax.broadcasted_iota(jnp.int32, square, 1)
    source_layer = jnp.sum(
        jnp.where(diagonal, jnp.broadcast_to(layer_ref[...], square), 0), axis=1, keepdims=True
    )
    source_layer = jnp.broadcast_to(jnp.concatenate([source_layer, source_layer], axis=0), (rows, width))
    up_own = jnp.where(
        layer >= source_layer, up_ref[...].reshape(rows, width).astype(jnp.float32), 0.0
    ).astype(jnp.bfloat16)
    down_own = jnp.where(
        layer <= source_layer, down_ref[...].reshape(rows, width).astype(jnp.float32), 0.0
    ).astype(jnp.bfloat16)
    up_all[0, me] = up_own
    own_down[...] = down_own

    @pl.when(jnp.logical_not(has_above))
    def _():
        up_next[...] = jnp.zeros_like(up_next)
        down_first[...] = jnp.zeros_like(down_first)
        part[0] = jnp.zeros_like(part[0])
        part[1] = jnp.zeros_like(part[1])

    peers = n - 1 + jnp.where(has_above, n // 2, 0) + jnp.where(has_below, n // 2, 0)
    pl.semaphore_wait(barrier, peers)

    def gather(k):
        return remote(
            up_all.at[0, me], up_all.at[0, me], up_ssem.at[0, k], up_rsem.at[0, me], layer, others[k]
        )

    def next_up():
        return remote(up_all.at[0, me], up_next, next_ssem, next_rsem, layer - 1, me)

    def first_down():
        return remote(own_down, down_first, first_ssem, first_rsem, layer - 1, me)

    def up_step(t, k):
        return remote(
            up_send.at[t], up_all.at[t + 1, me], up_ssem.at[t + 1, k], up_rsem.at[t + 1, me],
            layer + 1, like[k],
        )

    def relay(t, k):
        slot = up_all.at[t, like[k]]
        return remote(slot, slot, relay_ssem.at[t - 1, k], up_rsem.at[t, like[k]], layer, twin)

    def last_up():
        return remote(up_send.at[STEPS - 1], up_last, last_ssem, last_rsem, layer + 1, me)

    def part_step(t, k):
        return remote(
            part_send.at[t, k], part.at[t, chip], part_ssem.at[t, k], part_rsem.at[t, chip],
            layer - 1, like[k],
        )

    def twin_step(t, k):
        place = unlike[k] // 2
        return remote(
            twin_send.at[t, k], twin_part.at[t, place], twin_ssem.at[t, k], twin_rsem.at[t, place],
            layer, twin,
        )

    def last_part(k):
        return remote(
            last_send.at[k], last_in.at[me], last_part_ssem.at[k], last_part_rsem.at[me],
            layer, others[k],
        )

    def arrived(ref, rsem):
        remote(ref, ref, next_ssem, rsem, layer, me).wait_recv()

    for k in range(1, n):
        gather(k).start()

    @pl.when(has_below)
    def _():
        first_down().start()
        next_up().start()

    rank_index = lax.broadcasted_iota(jnp.int32, (sources, max_rank), 1)

    def coefficients(trace, factor, block):
        product = lax.dot_general(
            trace, factor.reshape(2 * max_rank, width), (((1,), (1,)), ((), ())),
            preferred_element_type=jnp.float32,
        )
        keep = rank_index < (max_rank // 4) * rank_ref[0, 0, block]
        real = product[:sources, :max_rank] - product[sources:, max_rank:]
        imag = product[:sources, max_rank:] + product[sources:, :max_rank]
        real = jnp.where(keep, real, 0.0)
        imag = jnp.where(keep, imag, 0.0)
        return jnp.concatenate(
            [jnp.concatenate([real, -imag], axis=1), jnp.concatenate([imag, real], axis=1)], axis=0
        ).astype(jnp.bfloat16)

    def expand(coef, factor):
        return jnp.dot(
            coef, factor.reshape(2 * max_rank, width), preferred_element_type=jnp.float32
        )

    load_v.wait()
    load_u.wait()

    for t in range(STEPS):
        held = 0 if t == 0 else jnp.where(has_below, t, 0)
        if t > 0:

            @pl.when(has_below)
            def _():
                for k in range(n // 2):
                    arrived(up_all.at[t, like[k]], up_rsem.at[t, like[k]])
                    relay(t, k).start()
                for k in range(n // 2):
                    arrived(up_all.at[t, unlike[k]], up_rsem.at[t, unlike[k]])

        else:
            for k in range(1, n):
                arrived(up_all.at[0, others[k]], up_rsem.at[0, others[k]])

            @pl.when(has_above)
            def _():
                arrived(up_next, next_rsem)

        total = up_next[...].astype(jnp.float32)
        for k in range(n):
            block = others[k]
            coef = coefficients(up_all[held, block], v_mem[block], block)
            total = total + expand(coef, u_mem[block])
        up_send[t] = total.astype(jnp.bfloat16)

        @pl.when(has_above)
        def _():
            if t < STEPS - 1:
                for k in reversed(range(n // 2)):
                    up_step(t, k).start()
            else:
                last_up().start()

        @pl.when(has_above)
        def _():
            if t == 0:
                arrived(down_first, first_rsem)
            else:
                for k in range(n // 2):
                    place = like[k] // 2
                    arrived(part.at[t - 1, place], part_rsem.at[t - 1, place])

        down = down_first[...]
        if t > 0:
            total = down.astype(jnp.float32)
            for k in range(n // 2):
                total = total + part[t - 1, like[k] // 2].astype(jnp.float32)
            down = total.astype(jnp.bfloat16)

        def piece(block):
            return expand(coefficients(down, u_mem[block], block), v_mem[block])

        if t < STEPS - 1:
            for k in range(n // 2):
                twin_send[t, k] = piece(unlike[k]).astype(jnp.bfloat16)
                twin_step(t, k).start()
            pieces = [piece(like[k]) for k in range(n // 2)]
            for k in range(n // 2):
                place = like[k] // 2
                arrived(twin_part.at[t, place], twin_rsem.at[t, place])
                part_send[t, k] = (pieces[k] + twin_part[t, place].astype(jnp.float32)).astype(
                    jnp.bfloat16
                )

            @pl.when(has_below)
            def _():
                for k in reversed(range(n // 2)):
                    part_step(t, k).start()

        else:
            for k in range(1, n):
                last_send[k] = piece(others[k]).astype(jnp.bfloat16)
                last_part(k).start()
            own_part = piece(me)

    total = own_down[...].astype(jnp.float32) + own_part
    for k in range(1, n):
        arrived(last_in.at[others[k]], last_part_rsem.at[others[k]])
        total = total + last_in[others[k]].astype(jnp.float32)
    down_done[...] = total.astype(jnp.bfloat16).reshape(2, sources, width)
    put_down = pltpu.make_async_copy(down_done, down_out.at[0], load_sem.at[0])
    put_down.start()

    @pl.when(has_below)
    def _():
        arrived(up_last, last_rsem)
        up_ref[...] = up_last[...].reshape(2, sources, width)

    @pl.when(jnp.logical_not(has_below))
    def _():
        up_ref[...] = up_all[0, me].reshape(2, sources, width)

    put_up = pltpu.make_async_copy(up_ref, up_out.at[0], load_sem.at[1])
    put_up.start()

    for k in range(1, n):
        gather(k).wait_send()
        last_part(k).wait_send()
    for t in range(STEPS - 1):
        for k in range(n // 2):
            twin_step(t, k).wait_send()

    @pl.when(has_below)
    def _():
        first_down().wait_send()
        next_up().wait_send()
        for t in range(STEPS - 1):
            for k in range(n // 2):
                part_step(t, k).wait_send()
                relay(t + 1, k).wait_send()

    @pl.when(has_above)
    def _():
        for t in range(STEPS - 1):
            for k in range(n // 2):
                up_step(t, k).wait_send()
        last_up().wait_send()

    put_down.wait()
    put_up.wait()


def solution(mesh):
    layers, n = mesh.shape["gz"], mesh.shape["xy"]

    def on_device(up_source, down_source, source_layer, u_factor, v_factor, block_rank):
        _, _, sources, width = up_source.shape
        rows = 2 * sources
        trace = (rows, width)
        anywhere = pl.BlockSpec(memory_space=pl.ANY)
        hbm = pl.BlockSpec(memory_space=pltpu.HBM)
        grant = (4 << 20) + 8 * u_factor.size
        dma = pltpu.SemaphoreType.DMA
        return pl.pallas_call(
            functools.partial(kernel, layers, n),
            out_shape=(
                jax.ShapeDtypeStruct(up_source.shape, jnp.bfloat16),
                jax.ShapeDtypeStruct(down_source.shape, jnp.bfloat16),
            ),
            in_specs=[hbm] * 6,
            out_specs=(anywhere, anywhere),
            scratch_shapes=[
                pltpu.VMEM((2, sources, width), jnp.bfloat16),
                pltpu.VMEM((2, sources, width), jnp.bfloat16),
                pltpu.VMEM((1, sources), jnp.int32),
                pltpu.SMEM(block_rank.shape, jnp.int32),
                pltpu.VMEM((2, sources, width), jnp.bfloat16),
                pltpu.VMEM(u_factor.shape[2:], jnp.bfloat16),
                pltpu.VMEM(v_factor.shape[2:], jnp.bfloat16),
                pltpu.VMEM((STEPS, n, *trace), jnp.bfloat16),
                pltpu.VMEM((STEPS, *trace), jnp.bfloat16),
                pltpu.VMEM(trace, jnp.bfloat16),
                pltpu.VMEM(trace, jnp.bfloat16),
                pltpu.VMEM(trace, jnp.bfloat16),
                pltpu.VMEM(trace, jnp.bfloat16),
                pltpu.VMEM((STEPS - 1, n // 2, *trace), jnp.bfloat16),
                pltpu.VMEM((STEPS - 1, n // 2, *trace), jnp.bfloat16),
                pltpu.VMEM((STEPS - 1, n // 2, *trace), jnp.bfloat16),
                pltpu.VMEM((STEPS - 1, n // 2, *trace), jnp.bfloat16),
                pltpu.VMEM((n, *trace), jnp.bfloat16),
                pltpu.VMEM((n, *trace), jnp.bfloat16),
                dma((6,)),
                dma((STEPS, n)),
                dma((STEPS, n)),
                dma,
                dma,
                dma,
                dma,
                dma,
                dma,
                dma((STEPS - 1, n // 2)),
                dma((STEPS - 1, n // 2)),
                dma((STEPS - 1, n // 2)),
                dma((STEPS - 1, n // 2)),
                dma((STEPS - 1, n // 2)),
                dma((n,)),
                dma((n,)),
            ],
            compiler_params=pltpu.CompilerParams(
                collective_id=0, has_side_effects=True, vmem_limit_bytes=grant
            ),
        )(up_source, down_source, source_layer.reshape(1, sources), u_factor, v_factor, block_rank)

    in_specs = (
        P("gz", None, None, "xy"),
        P("gz", None, None, "xy"),
        P(),
        P("gz", "xy", None, None, None, None),
        P("gz", "xy", None, None, None, None),
        P("gz", "xy", None),
    )
    out_specs = (P("gz", None, None, "xy"), P("gz", None, None, "xy"))
    return jax.shard_map(
        on_device, mesh=mesh, in_specs=in_specs, out_specs=out_specs, check_vma=False
    )
```

```python
import functools

import jax
import jax.numpy as jnp
from jax import lax
from jax.experimental import pallas as pl
from jax.experimental.pallas import tpu as pltpu
from jax.sharding import PartitionSpec as P

STEPS = 3
MESH = pl.DeviceIdType.MESH


def kernel(
    layers, n, up_hbm, down_hbm, layer_hbm, u_hbm, v_hbm, rank_hbm, up_out, down_out,
    up_ref, down_ref, layer_ref, rank_ref, down_done,
    u_mem, v_mem, up_all, up_send, up_next, up_last, own_down, down_first, part, part_send,
    twin_part, twin_send, last_in, last_send,
    load_sem, up_ssem, up_rsem, next_ssem, next_rsem, last_ssem, last_rsem,
    first_ssem, first_rsem, part_ssem, part_rsem,
    relay_ssem, twin_ssem, twin_rsem, last_part_ssem, last_part_rsem,
):
    layer = lax.axis_index("gz")
    me = lax.axis_index("xy")
    has_above = layer < layers - 1
    has_below = layer > 0
    rows, width = up_send.shape[1:]
    sources = rows // 2
    max_rank = u_mem.shape[2]
    others = [lax.rem(me + k, n) for k in range(n)]
    core = lax.rem(me, 2)
    twin = me + 1 - 2 * core
    like = [lax.rem(me + 2 * k, n) for k in range(n // 2)]
    unlike = [lax.rem(twin + 2 * k, n) for k in range(n // 2)]
    chip = me // 2

    def remote(src, dst, ssem, rsem, to_layer, to_block):
        return pltpu.make_async_remote_copy(
            src_ref=src, dst_ref=dst, send_sem=ssem, recv_sem=rsem,
            device_id={"gz": to_layer, "xy": to_block}, device_id_type=MESH,
        )

    load_u = pltpu.make_async_copy(u_hbm.at[0, 0], u_mem, load_sem.at[0])
    load_v = pltpu.make_async_copy(v_hbm.at[0, 0], v_mem, load_sem.at[1])
    small = [
        pltpu.make_async_copy(src, dst, load_sem.at[2 + i])
        for i, (src, dst) in enumerate(
            [(layer_hbm, layer_ref), (up_hbm.at[0], up_ref), (down_hbm.at[0], down_ref), (rank_hbm, rank_ref)]
        )
    ]
    for load in small:
        load.start()

    barrier = pltpu.get_barrier_semaphore()

    def greet(to_layer, to_block):
        pl.semaphore_signal(
            barrier, inc=1, device_id={"gz": to_layer, "xy": to_block}, device_id_type=MESH
        )

    for k in range(1, n):
        greet(layer, others[k])

    @pl.when(has_above)
    def _():
        for k in range(n // 2):
            greet(layer + 1, like[k])

    @pl.when(has_below)
    def _():
        for k in range(n // 2):
            greet(layer - 1, like[k])

    load_v.start()
    load_u.start()
    for load in small:
        load.wait()
    square = (sources, sources)
    diagonal = lax.broadcasted_iota(jnp.int32, square, 0) == lax.broadcasted_iota(jnp.int32, square, 1)
    source_layer = jnp.sum(
        jnp.where(diagonal, jnp.broadcast_to(layer_ref[...], square), 0), axis=1, keepdims=True
    )
    source_layer = jnp.broadcast_to(jnp.concatenate([source_layer, source_layer], axis=0), (rows, width))
    up_own = jnp.where(
        layer >= source_layer, up_ref[...].reshape(rows, width).astype(jnp.float32), 0.0
    ).astype(jnp.bfloat16)
    down_own = jnp.where(
        layer <= source_layer, down_ref[...].reshape(rows, width).astype(jnp.float32), 0.0
    ).astype(jnp.bfloat16)
    up_all[0, me] = up_own
    own_down[...] = down_own

    @pl.when(jnp.logical_not(has_above))
    def _():
        up_next[...] = jnp.zeros_like(up_next)
        down_first[...] = jnp.zeros_like(down_first)
        part[0] = jnp.zeros_like(part[0])
        part[1] = jnp.zeros_like(part[1])

    peers = n - 1 + jnp.where(has_above, n // 2, 0) + jnp.where(has_below, n // 2, 0)
    pl.semaphore_wait(barrier, peers)

    def gather(k):
        return remote(
            up_all.at[0, me], up_all.at[0, me], up_ssem.at[0, k], up_rsem.at[0, me], layer, others[k]
        )

    def next_up():
        return remote(up_all.at[0, me], up_next, next_ssem, next_rsem, layer - 1, me)

    def first_down():
        return remote(own_down, down_first, first_ssem, first_rsem, layer - 1, me)

    def up_step(t, k):
        return remote(
            up_send.at[t], up_all.at[t + 1, me], up_ssem.at[t + 1, k], up_rsem.at[t + 1, me],
            layer + 1, like[k],
        )

    def relay(t, k):
        slot = up_all.at[t, like[k]]
        return remote(slot, slot, relay_ssem.at[t - 1, k], up_rsem.at[t, like[k]], layer, twin)

    def last_up():
        return remote(up_send.at[STEPS - 1], up_last, last_ssem, last_rsem, layer + 1, me)

    def part_step(t, k):
        return remote(
            part_send.at[t, k], part.at[t, chip], part_ssem.at[t, k], part_rsem.at[t, chip],
            layer - 1, like[k],
        )

    def twin_step(t, k):
        place = unlike[k] // 2
        return remote(
            twin_send.at[t, k], twin_part.at[t, place], twin_ssem.at[t, k], twin_rsem.at[t, place],
            layer, twin,
        )

    def last_part(k):
        return remote(
            last_send.at[k], last_in.at[me], last_part_ssem.at[k], last_part_rsem.at[me],
            layer, others[k],
        )

    def arrived(ref, rsem):
        remote(ref, ref, next_ssem, rsem, layer, me).wait_recv()

    for k in range(1, n):
        gather(k).start()

    @pl.when(has_below)
    def _():
        first_down().start()
        next_up().start()

    rank_index = lax.broadcasted_iota(jnp.int32, (sources, max_rank), 1)

    def coefficients(trace, factor, block):
        product = lax.dot_general(
            trace, factor.reshape(2 * max_rank, width), (((1,), (1,)), ((), ())),
            preferred_element_type=jnp.float32,
        )
        keep = rank_index < (max_rank // 4) * rank_ref[0, 0, block]
        real = product[:sources, :max_rank] - product[sources:, max_rank:]
        imag = product[:sources, max_rank:] + product[sources:, :max_rank]
        real = jnp.where(keep, real, 0.0)
        imag = jnp.where(keep, imag, 0.0)
        return jnp.concatenate(
            [jnp.concatenate([real, -imag], axis=1), jnp.concatenate([imag, real], axis=1)], axis=0
        ).astype(jnp.bfloat16)

    def expand(coef, factor):
        return jnp.dot(
            coef, factor.reshape(2 * max_rank, width), preferred_element_type=jnp.float32
        )

    load_v.wait()
    load_u.wait()

    for t in range(STEPS):
        held = 0 if t == 0 else jnp.where(has_below, t, 0)
        if t > 0:

            @pl.when(has_below)
            def _():
                for k in range(n // 2):
                    arrived(up_all.at[t, like[k]], up_rsem.at[t, like[k]])
                    relay(t, k).start()
                for k in range(n // 2):
                    arrived(up_all.at[t, unlike[k]], up_rsem.at[t, unlike[k]])

        else:
            for k in range(1, n):
                arrived(up_all.at[0, others[k]], up_rsem.at[0, others[k]])

            @pl.when(has_above)
            def _():
                arrived(up_next, next_rsem)

        total = up_next[...].astype(jnp.float32)
        for k in range(n):
            block = others[k]
            coef = coefficients(up_all[held, block], v_mem[block], block)
            total = total + expand(coef, u_mem[block])
        up_send[t] = total.astype(jnp.bfloat16)

        @pl.when(has_above)
        def _():
            if t < STEPS - 1:
                for k in reversed(range(n // 2)):
                    up_step(t, k).start()
            else:
                last_up().start()

        @pl.when(has_above)
        def _():
            if t == 0:
                arrived(down_first, first_rsem)
            else:
                for k in range(n // 2):
                    place = like[k] // 2
                    arrived(part.at[t - 1, place], part_rsem.at[t - 1, place])

        down = down_first[...]
        if t > 0:
            total = down.astype(jnp.float32)
            for k in range(n // 2):
                total = total + part[t - 1, like[k] // 2].astype(jnp.float32)
            down = total.astype(jnp.bfloat16)

        def piece(block):
            return expand(coefficients(down, u_mem[block], block), v_mem[block])

        if t < STEPS - 1:
            for k in range(n // 2):
                twin_send[t, k] = piece(unlike[k]).astype(jnp.bfloat16)
                twin_step(t, k).start()
            pieces = [piece(like[k]) for k in range(n // 2)]
            for k in range(n // 2):
                place = like[k] // 2
                arrived(twin_part.at[t, place], twin_rsem.at[t, place])
                part_send[t, k] = (pieces[k] + twin_part[t, place].astype(jnp.float32)).astype(
                    jnp.bfloat16
                )

            @pl.when(has_below)
            def _():
                for k in reversed(range(n // 2)):
                    part_step(t, k).start()

        else:
            for k in range(1, n):
                last_send[k] = piece(others[k]).astype(jnp.bfloat16)
                last_part(k).start()
            own_part = piece(me)

    total = own_down[...].astype(jnp.float32) + own_part
    for k in range(1, n):
        arrived(last_in.at[others[k]], last_part_rsem.at[others[k]])
        total = total + last_in[others[k]].astype(jnp.float32)
    down_done[...] = total.astype(jnp.bfloat16).reshape(2, sources, width)
    put_down = pltpu.make_async_copy(down_done, down_out.at[0], load_sem.at[0])
    put_down.start()

    @pl.when(has_below)
    def _():
        arrived(up_last, last_rsem)
        up_ref[...] = up_last[...].reshape(2, sources, width)

    @pl.when(jnp.logical_not(has_below))
    def _():
        up_ref[...] = up_all[0, me].reshape(2, sources, width)

    put_up = pltpu.make_async_copy(up_ref, up_out.at[0], load_sem.at[1])
    put_up.start()

    for k in range(1, n):
        gather(k).wait_send()
        last_part(k).wait_send()
    for t in range(STEPS - 1):
        for k in range(n // 2):
            twin_step(t, k).wait_send()

    @pl.when(has_below)
    def _():
        first_down().wait_send()
        next_up().wait_send()
        for t in range(STEPS - 1):
            for k in range(n // 2):
                part_step(t, k).wait_send()
                relay(t + 1, k).wait_send()

    @pl.when(has_above)
    def _():
        for t in range(STEPS - 1):
            for k in range(n // 2):
                up_step(t, k).wait_send()
        last_up().wait_send()

    put_down.wait()
    put_up.wait()


def solution(mesh):
    layers, n = mesh.shape["gz"], mesh.shape["xy"]

    def on_device(up_source, down_source, source_layer, u_factor, v_factor, block_rank):
        _, _, sources, width = up_source.shape
        rows = 2 * sources
        trace = (rows, width)
        anywhere = pl.BlockSpec(memory_space=pl.ANY)
        hbm = pl.BlockSpec(memory_space=pltpu.HBM)
        dma = pltpu.SemaphoreType.DMA
        return pl.pallas_call(
            functools.partial(kernel, layers, n),
            out_shape=(
                jax.ShapeDtypeStruct(up_source.shape, jnp.bfloat16),
                jax.ShapeDtypeStruct(down_source.shape, jnp.bfloat16),
            ),
            in_specs=[hbm] * 6,
            out_specs=(anywhere, anywhere),
            scratch_shapes=[
                pltpu.VMEM((2, sources, width), jnp.bfloat16),
                pltpu.VMEM((2, sources, width), jnp.bfloat16),
                pltpu.VMEM((1, sources), jnp.int32),
                pltpu.SMEM(block_rank.shape, jnp.int32),
                pltpu.VMEM((2, sources, width), jnp.bfloat16),
                pltpu.VMEM(u_factor.shape[2:], jnp.bfloat16),
                pltpu.VMEM(v_factor.shape[2:], jnp.bfloat16),
                pltpu.VMEM((STEPS, n, *trace), jnp.bfloat16),
                pltpu.VMEM((STEPS, *trace), jnp.bfloat16),
                pltpu.VMEM(trace, jnp.bfloat16),
                pltpu.VMEM(trace, jnp.bfloat16),
                pltpu.VMEM(trace, jnp.bfloat16),
                pltpu.VMEM(trace, jnp.bfloat16),
                pltpu.VMEM((STEPS - 1, n // 2, *trace), jnp.bfloat16),
                pltpu.VMEM((STEPS - 1, n // 2, *trace), jnp.bfloat16),
                pltpu.VMEM((STEPS - 1, n // 2, *trace), jnp.bfloat16),
                pltpu.VMEM((STEPS - 1, n // 2, *trace), jnp.bfloat16),
                pltpu.VMEM((n, *trace), jnp.bfloat16),
                pltpu.VMEM((n, *trace), jnp.bfloat16),
                dma((6,)),
                dma((STEPS, n)),
                dma((STEPS, n)),
                dma,
                dma,
                dma,
                dma,
                dma,
                dma,
                dma((STEPS - 1, n // 2)),
                dma((STEPS - 1, n // 2)),
                dma((STEPS - 1, n // 2)),
                dma((STEPS - 1, n // 2)),
                dma((STEPS - 1, n // 2)),
                dma((n,)),
                dma((n,)),
            ],
            compiler_params=pltpu.CompilerParams(
                collective_id=0, has_side_effects=True
            ),
        )(up_source, down_source, source_layer.reshape(1, sources), u_factor, v_factor, block_rank)

    in_specs = (
        P("gz", None, None, "xy"),
        P("gz", None, None, "xy"),
        P(),
        P("gz", "xy", None, None, None, None),
        P("gz", "xy", None, None, None, None),
        P("gz", "xy", None),
    )
    out_specs = (P("gz", None, None, "xy"), P("gz", None, None, "xy"))
    return jax.shard_map(
        on_device, mesh=mesh, in_specs=in_specs, out_specs=out_specs, check_vma=False
    )
```

```python
import functools

import jax
import jax.numpy as jnp
from jax import lax
from jax.experimental import pallas as pl
from jax.experimental.pallas import tpu as pltpu
from jax.sharding import PartitionSpec as P

STEPS = 3
MESH = pl.DeviceIdType.MESH


def kernel(
    layers, n, up_hbm, down_hbm, layer_hbm, u_hbm, v_hbm, rank_hbm, up_out, down_out,
    up_ref, down_ref, layer_ref, rank_ref, down_done,
    u_mem, v_mem, up_all, up_send, up_next, up_last, own_down, down_first, part, part_send,
    twin_part, twin_send, last_in, last_send,
    load_sem, up_ssem, up_rsem, next_ssem, next_rsem, last_ssem, last_rsem,
    first_ssem, first_rsem, part_ssem, part_rsem,
    relay_ssem, twin_ssem, twin_rsem, last_part_ssem, last_part_rsem,
):
    layer = lax.axis_index("gz")
    me = lax.axis_index("xy")
    has_above = layer < layers - 1
    has_below = layer > 0
    rows, width = up_send.shape[1:]
    sources = rows // 2
    max_rank = u_mem.shape[2]
    others = [lax.rem(me + k, n) for k in range(n)]
    core = lax.rem(me, 2)
    twin = me + 1 - 2 * core
    like = [lax.rem(me + 2 * k, n) for k in range(n // 2)]
    unlike = [lax.rem(twin + 2 * k, n) for k in range(n // 2)]
    chip = me // 2

    def remote(src, dst, ssem, rsem, to_layer, to_block):
        return pltpu.make_async_remote_copy(
            src_ref=src, dst_ref=dst, send_sem=ssem, recv_sem=rsem,
            device_id={"gz": to_layer, "xy": to_block}, device_id_type=MESH,
        )

    load_u = pltpu.make_async_copy(u_hbm.at[0, 0], u_mem, load_sem.at[0])
    load_v = pltpu.make_async_copy(v_hbm.at[0, 0], v_mem, load_sem.at[1])
    small = [
        pltpu.make_async_copy(src, dst, load_sem.at[2 + i])
        for i, (src, dst) in enumerate(
            [(layer_hbm, layer_ref), (up_hbm.at[0], up_ref), (down_hbm.at[0], down_ref), (rank_hbm, rank_ref)]
        )
    ]
    for load in small:
        load.start()

    barrier = pltpu.get_barrier_semaphore()

    def greet(to_layer, to_block):
        pl.semaphore_signal(
            barrier, inc=1, device_id={"gz": to_layer, "xy": to_block}, device_id_type=MESH
        )

    for k in range(1, n):
        greet(layer, others[k])

    @pl.when(has_above)
    def _():
        for k in range(n // 2):
            greet(layer + 1, like[k])

    @pl.when(has_below)
    def _():
        for k in range(n // 2):
            greet(layer - 1, like[k])

    load_v.start()
    load_u.start()
    for load in small:
        load.wait()
    square = (sources, sources)
    diagonal = lax.broadcasted_iota(jnp.int32, square, 0) == lax.broadcasted_iota(jnp.int32, square, 1)
    source_layer = jnp.sum(
        jnp.where(diagonal, jnp.broadcast_to(layer_ref[...], square), 0), axis=1, keepdims=True
    )
    source_layer = jnp.broadcast_to(jnp.concatenate([source_layer, source_layer], axis=0), (rows, width))
    up_own = jnp.where(
        layer >= source_layer, up_ref[...].reshape(rows, width).astype(jnp.float32), 0.0
    ).astype(jnp.bfloat16)
    down_own = jnp.where(
        layer <= source_layer, down_ref[...].reshape(rows, width).astype(jnp.float32), 0.0
    ).astype(jnp.bfloat16)
    up_all[0, me] = up_own
    own_down[...] = down_own

    @pl.when(jnp.logical_not(has_above))
    def _():
        up_next[...] = jnp.zeros_like(up_next)
        down_first[...] = jnp.zeros_like(down_first)
        part[0] = jnp.zeros_like(part[0])
        part[1] = jnp.zeros_like(part[1])

    peers = n - 1 + jnp.where(has_above, n // 2, 0) + jnp.where(has_below, n // 2, 0)
    pl.semaphore_wait(barrier, peers)

    def gather(k):
        return remote(
            up_all.at[0, me], up_all.at[0, me], up_ssem.at[0, k], up_rsem.at[0, me], layer, others[k]
        )

    def next_up():
        return remote(up_all.at[0, me], up_next, next_ssem, next_rsem, layer - 1, me)

    def first_down():
        return remote(own_down, down_first, first_ssem, first_rsem, layer - 1, me)

    def up_step(t, k):
        return remote(
            up_send.at[t], up_all.at[t + 1, me], up_ssem.at[t + 1, k], up_rsem.at[t + 1, me],
            layer + 1, like[k],
        )

    def relay(t, k):
        slot = up_all.at[t, like[k]]
        return remote(slot, slot, relay_ssem.at[t - 1, k], up_rsem.at[t, like[k]], layer, twin)

    def last_up():
        return remote(up_send.at[STEPS - 1], up_last, last_ssem, last_rsem, layer + 1, me)

    def part_step(t, k):
        return remote(
            part_send.at[t, k], part.at[t, chip], part_ssem.at[t, k], part_rsem.at[t, chip],
            layer - 1, like[k],
        )

    def twin_step(t, k):
        place = unlike[k] // 2
        return remote(
            twin_send.at[t, k], twin_part.at[t, place], twin_ssem.at[t, k], twin_rsem.at[t, place],
            layer, twin,
        )

    def last_part(k):
        return remote(
            last_send.at[k], last_in.at[me], last_part_ssem.at[k], last_part_rsem.at[me],
            layer, others[k],
        )

    def arrived(ref, rsem):
        remote(ref, ref, next_ssem, rsem, layer, me).wait_recv()

    for k in range(1, n):
        gather(k).start()

    @pl.when(has_below)
    def _():
        first_down().start()
        next_up().start()

    rank_index = lax.broadcasted_iota(jnp.int32, (sources, max_rank), 1)

    def coefficients(trace, factor, block):
        product = lax.dot_general(
            trace, factor.reshape(2 * max_rank, width), (((1,), (1,)), ((), ())),
            preferred_element_type=jnp.float32,
        )
        keep = rank_index < (max_rank // 4) * rank_ref[0, 0, block]
        real = product[:sources, :max_rank] - product[sources:, max_rank:]
        imag = product[:sources, max_rank:] + product[sources:, :max_rank]
        real = jnp.where(keep, real, 0.0)
        imag = jnp.where(keep, imag, 0.0)
        return jnp.concatenate(
            [jnp.concatenate([real, -imag], axis=1), jnp.concatenate([imag, real], axis=1)], axis=0
        ).astype(jnp.bfloat16)

    def expand(coef, factor):
        return jnp.dot(
            coef, factor.reshape(2 * max_rank, width), preferred_element_type=jnp.float32
        )

    load_v.wait()
    load_u.wait()

    def wait_blocks(t, blocks):
        for block in blocks:
            arrived(up_all.at[t, block], up_rsem.at[t, block])

    for t in range(STEPS):
        last = t == STEPS - 1
        held = 0 if t == 0 else jnp.where(has_below, t, 0)

        def rise(block):
            return expand(coefficients(up_all[held, block], v_mem[block], block), u_mem[block])

        def piece(block):
            return expand(coefficients(down, u_mem[block], block), v_mem[block])

        if t > 0:

            @pl.when(has_below)
            def _():
                for k in range(n // 2):
                    wait_blocks(t, [like[k]])
                    relay(t, k).start()

        @pl.when(has_above)
        def _():
            if t == 0:
                arrived(down_first, first_rsem)
            else:
                for k in range(n // 2):
                    place = like[k] // 2
                    arrived(part.at[t - 1, place], part_rsem.at[t - 1, place])

        down = down_first[...]
        if t > 0:
            total = down.astype(jnp.float32)
            for k in range(n // 2):
                total = total + part[t - 1, like[k] // 2].astype(jnp.float32)
            down = total.astype(jnp.bfloat16)

        if last:
            for k in range(1, n):
                last_send[k] = piece(others[k]).astype(jnp.bfloat16)
                last_part(k).start()
        else:
            for k in range(n // 2):
                twin_send[t, k] = piece(unlike[k]).astype(jnp.bfloat16)
                twin_step(t, k).start()

        if t == 0:
            wait_blocks(0, like[1:])
        total = sum([rise(block) for block in like])
        if t == 0:
            wait_blocks(0, unlike)

            @pl.when(has_above)
            def _():
                arrived(up_next, next_rsem)

        else:

            @pl.when(has_below)
            def _():
                wait_blocks(t, unlike)

        total = total + sum([rise(block) for block in unlike])
        up_send[t] = (up_next[...].astype(jnp.float32) + total).astype(jnp.bfloat16)

        @pl.when(has_above)
        def _():
            if last:
                last_up().start()
            else:
                for k in reversed(range(n // 2)):
                    up_step(t, k).start()

        if last:
            own_part = piece(me)
        else:
            pieces = [piece(block) for block in like]
            for k in range(n // 2):
                place = like[k] // 2
                arrived(twin_part.at[t, place], twin_rsem.at[t, place])
                part_send[t, k] = (pieces[k] + twin_part[t, place].astype(jnp.float32)).astype(
                    jnp.bfloat16
                )

            @pl.when(has_below)
            def _():
                for k in reversed(range(n // 2)):
                    part_step(t, k).start()

    total = own_down[...].astype(jnp.float32) + own_part
    for k in range(1, n):
        arrived(last_in.at[others[k]], last_part_rsem.at[others[k]])
        total = total + last_in[others[k]].astype(jnp.float32)
    down_done[...] = total.astype(jnp.bfloat16).reshape(2, sources, width)
    put_down = pltpu.make_async_copy(down_done, down_out.at[0], load_sem.at[0])
    put_down.start()

    @pl.when(has_below)
    def _():
        arrived(up_last, last_rsem)
        up_ref[...] = up_last[...].reshape(2, sources, width)

    @pl.when(jnp.logical_not(has_below))
    def _():
        up_ref[...] = up_all[0, me].reshape(2, sources, width)

    put_up = pltpu.make_async_copy(up_ref, up_out.at[0], load_sem.at[1])
    put_up.start()

    for k in range(1, n):
        gather(k).wait_send()
        last_part(k).wait_send()
    for t in range(STEPS - 1):
        for k in range(n // 2):
            twin_step(t, k).wait_send()

    @pl.when(has_below)
    def _():
        first_down().wait_send()
        next_up().wait_send()
        for t in range(STEPS - 1):
            for k in range(n // 2):
                part_step(t, k).wait_send()
                relay(t + 1, k).wait_send()

    @pl.when(has_above)
    def _():
        for t in range(STEPS - 1):
            for k in range(n // 2):
                up_step(t, k).wait_send()
        last_up().wait_send()

    put_down.wait()
    put_up.wait()


def solution(mesh):
    layers, n = mesh.shape["gz"], mesh.shape["xy"]

    def on_device(up_source, down_source, source_layer, u_factor, v_factor, block_rank):
        _, _, sources, width = up_source.shape
        rows = 2 * sources
        trace = (rows, width)
        anywhere = pl.BlockSpec(memory_space=pl.ANY)
        hbm = pl.BlockSpec(memory_space=pltpu.HBM)
        dma = pltpu.SemaphoreType.DMA
        return pl.pallas_call(
            functools.partial(kernel, layers, n),
            out_shape=(
                jax.ShapeDtypeStruct(up_source.shape, jnp.bfloat16),
                jax.ShapeDtypeStruct(down_source.shape, jnp.bfloat16),
            ),
            in_specs=[hbm] * 6,
            out_specs=(anywhere, anywhere),
            scratch_shapes=[
                pltpu.VMEM((2, sources, width), jnp.bfloat16),
                pltpu.VMEM((2, sources, width), jnp.bfloat16),
                pltpu.VMEM((1, sources), jnp.int32),
                pltpu.SMEM(block_rank.shape, jnp.int32),
                pltpu.VMEM((2, sources, width), jnp.bfloat16),
                pltpu.VMEM(u_factor.shape[2:], jnp.bfloat16),
                pltpu.VMEM(v_factor.shape[2:], jnp.bfloat16),
                pltpu.VMEM((STEPS, n, *trace), jnp.bfloat16),
                pltpu.VMEM((STEPS, *trace), jnp.bfloat16),
                pltpu.VMEM(trace, jnp.bfloat16),
                pltpu.VMEM(trace, jnp.bfloat16),
                pltpu.VMEM(trace, jnp.bfloat16),
                pltpu.VMEM(trace, jnp.bfloat16),
                pltpu.VMEM((STEPS - 1, n // 2, *trace), jnp.bfloat16),
                pltpu.VMEM((STEPS - 1, n // 2, *trace), jnp.bfloat16),
                pltpu.VMEM((STEPS - 1, n // 2, *trace), jnp.bfloat16),
                pltpu.VMEM((STEPS - 1, n // 2, *trace), jnp.bfloat16),
                pltpu.VMEM((n, *trace), jnp.bfloat16),
                pltpu.VMEM((n, *trace), jnp.bfloat16),
                dma((6,)),
                dma((STEPS, n)),
                dma((STEPS, n)),
                dma,
                dma,
                dma,
                dma,
                dma,
                dma,
                dma((STEPS - 1, n // 2)),
                dma((STEPS - 1, n // 2)),
                dma((STEPS - 1, n // 2)),
                dma((STEPS - 1, n // 2)),
                dma((STEPS - 1, n // 2)),
                dma((n,)),
                dma((n,)),
            ],
            compiler_params=pltpu.CompilerParams(
                collective_id=0, has_side_effects=True
            ),
        )(up_source, down_source, source_layer.reshape(1, sources), u_factor, v_factor, block_rank)

    in_specs = (
        P("gz", None, None, "xy"),
        P("gz", None, None, "xy"),
        P(),
        P("gz", "xy", None, None, None, None),
        P("gz", "xy", None, None, None, None),
        P("gz", "xy", None),
    )
    out_specs = (P("gz", None, None, "xy"), P("gz", None, None, "xy"))
    return jax.shard_map(
        on_device, mesh=mesh, in_specs=in_specs, out_specs=out_specs, check_vma=False
    )
```

```python
import functools

import jax
import jax.numpy as jnp
from jax import lax
from jax.experimental import pallas as pl
from jax.experimental.pallas import tpu as pltpu
from jax.sharding import PartitionSpec as P

STEPS = 3
MESH = pl.DeviceIdType.MESH


def kernel(
    layers, n, up_hbm, down_hbm, layer_hbm, u_hbm, v_hbm, rank_hbm, up_out, down_out,
    up_ref, down_ref, layer_ref, rank_ref, down_done,
    u_mem, v_mem, up_all, up_send, up_next, up_last, own_down, down_first, part, part_send,
    twin_part, twin_send, last_in, last_send,
    load_sem, up_ssem, up_rsem, next_ssem, next_rsem, last_ssem, last_rsem,
    first_ssem, first_rsem, part_ssem, part_rsem,
    relay_ssem, twin_ssem, twin_rsem, last_part_ssem, last_part_rsem,
):
    layer = lax.axis_index("gz")
    me = lax.axis_index("xy")
    has_above = layer < layers - 1
    has_below = layer > 0
    rows, width = up_send.shape[1:]
    sources = rows // 2
    max_rank = u_mem.shape[2]
    others = [lax.rem(me + k, n) for k in range(n)]
    core = lax.rem(me, 2)
    twin = me + 1 - 2 * core
    like = [lax.rem(me + 2 * k, n) for k in range(n // 2)]
    unlike = [lax.rem(twin + 2 * k, n) for k in range(n // 2)]
    chip = me // 2

    def remote(src, dst, ssem, rsem, to_layer, to_block):
        return pltpu.make_async_remote_copy(
            src_ref=src, dst_ref=dst, send_sem=ssem, recv_sem=rsem,
            device_id={"gz": to_layer, "xy": to_block}, device_id_type=MESH,
        )

    load_u = pltpu.make_async_copy(u_hbm.at[0, 0], u_mem, load_sem.at[0])
    load_v = pltpu.make_async_copy(v_hbm.at[0, 0], v_mem, load_sem.at[1])
    small = [
        pltpu.make_async_copy(src, dst, load_sem.at[2 + i])
        for i, (src, dst) in enumerate(
            [(layer_hbm, layer_ref), (up_hbm.at[0], up_ref), (down_hbm.at[0], down_ref), (rank_hbm, rank_ref)]
        )
    ]
    for load in small:
        load.start()

    barrier = pltpu.get_barrier_semaphore()

    def greet(to_layer, to_block):
        pl.semaphore_signal(
            barrier, inc=1, device_id={"gz": to_layer, "xy": to_block}, device_id_type=MESH
        )

    for k in range(1, n):
        greet(layer, others[k])

    @pl.when(has_above)
    def _():
        for k in range(n // 2):
            greet(layer + 1, like[k])

    @pl.when(has_below)
    def _():
        for k in range(n // 2):
            greet(layer - 1, like[k])

    load_v.start()
    load_u.start()
    for load in small:
        load.wait()
    square = (sources, sources)
    diagonal = lax.broadcasted_iota(jnp.int32, square, 0) == lax.broadcasted_iota(jnp.int32, square, 1)
    source_layer = jnp.sum(
        jnp.where(diagonal, jnp.broadcast_to(layer_ref[...], square), 0), axis=1, keepdims=True
    )
    source_layer = jnp.broadcast_to(jnp.concatenate([source_layer, source_layer], axis=0), (rows, width))
    up_own = jnp.where(
        layer >= source_layer, up_ref[...].reshape(rows, width).astype(jnp.float32), 0.0
    ).astype(jnp.bfloat16)
    down_own = jnp.where(
        layer <= source_layer, down_ref[...].reshape(rows, width).astype(jnp.float32), 0.0
    ).astype(jnp.bfloat16)
    up_all[0, me] = up_own
    own_down[...] = down_own

    @pl.when(jnp.logical_not(has_above))
    def _():
        up_next[...] = jnp.zeros_like(up_next)
        down_first[...] = jnp.zeros_like(down_first)
        part[0] = jnp.zeros_like(part[0])
        part[1] = jnp.zeros_like(part[1])

    peers = n - 1 + jnp.where(has_above, n // 2, 0) + jnp.where(has_below, n // 2, 0)
    pl.semaphore_wait(barrier, peers)

    def gather(k):
        return remote(
            up_all.at[0, me], up_all.at[0, me], up_ssem.at[0, k], up_rsem.at[0, me], layer, others[k]
        )

    def next_up():
        return remote(up_all.at[0, me], up_next, next_ssem, next_rsem, layer - 1, me)

    def first_down():
        return remote(own_down, down_first, first_ssem, first_rsem, layer - 1, me)

    def up_step(t, k):
        return remote(
            up_send.at[t], up_all.at[t + 1, me], up_ssem.at[t + 1, k], up_rsem.at[t + 1, me],
            layer + 1, like[k],
        )

    def relay(t, k):
        slot = up_all.at[t, like[k]]
        return remote(slot, slot, relay_ssem.at[t - 1, k], up_rsem.at[t, like[k]], layer, twin)

    def last_up():
        return remote(up_send.at[STEPS - 1], up_last, last_ssem, last_rsem, layer + 1, me)

    def part_step(t, k):
        return remote(
            part_send.at[t, k], part.at[t, chip], part_ssem.at[t, k], part_rsem.at[t, chip],
            layer - 1, like[k],
        )

    def twin_step(t, k):
        place = unlike[k] // 2
        return remote(
            twin_send.at[t, k], twin_part.at[t, place], twin_ssem.at[t, k], twin_rsem.at[t, place],
            layer, twin,
        )

    def last_part(k):
        return remote(
            last_send.at[k], last_in.at[me], last_part_ssem.at[k], last_part_rsem.at[me],
            layer, others[k],
        )

    def arrived(ref, rsem):
        remote(ref, ref, next_ssem, rsem, layer, me).wait_recv()

    for k in range(1, n):
        gather(k).start()

    @pl.when(has_below)
    def _():
        first_down().start()
        next_up().start()

    rank_index = lax.broadcasted_iota(jnp.int32, (sources, max_rank), 1)

    def coefficients(trace, factor, block):
        product = lax.dot_general(
            trace, factor.reshape(2 * max_rank, width), (((1,), (1,)), ((), ())),
            preferred_element_type=jnp.float32,
        )
        keep = rank_index < (max_rank // 4) * rank_ref[0, 0, block]
        real = product[:sources, :max_rank] - product[sources:, max_rank:]
        imag = product[:sources, max_rank:] + product[sources:, :max_rank]
        real = jnp.where(keep, real, 0.0)
        imag = jnp.where(keep, imag, 0.0)
        return jnp.concatenate(
            [jnp.concatenate([real, -imag], axis=1), jnp.concatenate([imag, real], axis=1)], axis=0
        ).astype(jnp.bfloat16)

    def expand(coef, factor):
        return jnp.dot(
            coef, factor.reshape(2 * max_rank, width), preferred_element_type=jnp.float32
        )

    load_v.wait()
    load_u.wait()

    def wait_blocks(t, blocks):
        for block in blocks:
            arrived(up_all.at[t, block], up_rsem.at[t, block])

    for t in range(STEPS):
        last = t == STEPS - 1
        held = 0 if t == 0 else jnp.where(has_below, t, 0)

        def rise(block):
            return expand(coefficients(up_all[held, block], v_mem[block], block), u_mem[block])

        def piece(block):
            return expand(coefficients(down, u_mem[block], block), v_mem[block])

        if t > 0:

            @pl.when(has_below)
            def _():
                for k in range(n // 2):
                    wait_blocks(t, [like[k]])
                    relay(t, k).start()

        @pl.when(has_above)
        def _():
            if t == 0:
                arrived(down_first, first_rsem)
            else:
                for k in range(n // 2):
                    place = like[k] // 2
                    arrived(part.at[t - 1, place], part_rsem.at[t - 1, place])

        down = down_first[...]
        if t > 0:
            total = down.astype(jnp.float32)
            for k in range(n // 2):
                total = total + part[t - 1, like[k] // 2].astype(jnp.float32)
            down = total.astype(jnp.bfloat16)

        if last:
            for k in range(1, n):
                last_send[k] = piece(others[k]).astype(jnp.bfloat16)
                last_part(k).start()
        else:
            for k in range(n // 2):
                twin_send[t, k] = piece(unlike[k]).astype(jnp.bfloat16)
                twin_step(t, k).start()

        if t == 0:
            wait_blocks(0, like[1:])
        total = sum([rise(block) for block in like])
        if t == 0:
            wait_blocks(0, unlike)

            @pl.when(has_above)
            def _():
                arrived(up_next, next_rsem)

        else:

            @pl.when(has_below)
            def _():
                wait_blocks(t, unlike)

        total = total + sum([rise(block) for block in unlike])
        up_send[t] = (up_next[...].astype(jnp.float32) + total).astype(jnp.bfloat16)

        @pl.when(has_above)
        def _():
            if last:
                last_up().start()
            else:
                for k in reversed(range(n // 2)):
                    up_step(t, k).start()

        if last:
            own_part = piece(me)
        else:
            pieces = [piece(block) for block in like]
            for k in range(n // 2):
                place = like[k] // 2
                arrived(twin_part.at[t, place], twin_rsem.at[t, place])
                part_send[t, k] = (pieces[k] + twin_part[t, place].astype(jnp.float32)).astype(
                    jnp.bfloat16
                )

            @pl.when(has_below)
            def _():
                for k in reversed(range(n // 2)):
                    part_step(t, k).start()

    total = own_down[...].astype(jnp.float32) + own_part
    for k in range(1, n):
        arrived(last_in.at[others[k]], last_part_rsem.at[others[k]])
        total = total + last_in[others[k]].astype(jnp.float32)
    down_done[...] = total.astype(jnp.bfloat16).reshape(2, sources, width)
    put_down = pltpu.make_async_copy(down_done, down_out.at[0], load_sem.at[0])
    put_down.start()

    @pl.when(has_below)
    def _():
        arrived(up_last, last_rsem)
        up_ref[...] = up_last[...].reshape(2, sources, width)

    @pl.when(jnp.logical_not(has_below))
    def _():
        up_ref[...] = up_all[0, me].reshape(2, sources, width)

    put_up = pltpu.make_async_copy(up_ref, up_out.at[0], load_sem.at[1])
    put_up.start()

    for k in range(1, n):
        gather(k).wait_send()
        last_part(k).wait_send()
    for t in range(STEPS - 1):
        for k in range(n // 2):
            twin_step(t, k).wait_send()

    @pl.when(has_below)
    def _():
        first_down().wait_send()
        next_up().wait_send()
        for t in range(STEPS - 1):
            for k in range(n // 2):
                part_step(t, k).wait_send()
                relay(t + 1, k).wait_send()

    @pl.when(has_above)
    def _():
        for t in range(STEPS - 1):
            for k in range(n // 2):
                up_step(t, k).wait_send()
        last_up().wait_send()

    put_down.wait()
    put_up.wait()


def hand_over(up_ref, down_ref, up_out, down_out, up_mem, down_mem, sems):
    pairs = [(up_ref, up_mem, up_out), (down_ref, down_mem, down_out)]
    loads = [pltpu.make_async_copy(src, mem, sems.at[0, i]) for i, (src, mem, _) in enumerate(pairs)]
    stores = [pltpu.make_async_copy(mem, dst, sems.at[1, i]) for i, (_, mem, dst) in enumerate(pairs)]
    for load in loads:
        load.start()
    for load, store in zip(loads, stores):
        load.wait()
        store.start()
    for store in stores:
        store.wait()


def solution(mesh):
    layers, n = mesh.shape["gz"], mesh.shape["xy"]

    def on_device(up_source, down_source, source_layer, u_factor, v_factor, block_rank):
        _, _, sources, width = up_source.shape
        rows = 2 * sources
        trace = (rows, width)
        anywhere = pl.BlockSpec(memory_space=pl.ANY)
        hbm = pl.BlockSpec(memory_space=pltpu.HBM)
        dma = pltpu.SemaphoreType.DMA
        traces = pl.pallas_call(
            functools.partial(kernel, layers, n),
            out_shape=(
                jax.ShapeDtypeStruct(up_source.shape, jnp.bfloat16),
                jax.ShapeDtypeStruct(down_source.shape, jnp.bfloat16),
            ),
            in_specs=[hbm] * 6,
            out_specs=(anywhere, anywhere),
            scratch_shapes=[
                pltpu.VMEM((2, sources, width), jnp.bfloat16),
                pltpu.VMEM((2, sources, width), jnp.bfloat16),
                pltpu.VMEM((1, sources), jnp.int32),
                pltpu.SMEM(block_rank.shape, jnp.int32),
                pltpu.VMEM((2, sources, width), jnp.bfloat16),
                pltpu.VMEM(u_factor.shape[2:], jnp.bfloat16),
                pltpu.VMEM(v_factor.shape[2:], jnp.bfloat16),
                pltpu.VMEM((STEPS, n, *trace), jnp.bfloat16),
                pltpu.VMEM((STEPS, *trace), jnp.bfloat16),
                pltpu.VMEM(trace, jnp.bfloat16),
                pltpu.VMEM(trace, jnp.bfloat16),
                pltpu.VMEM(trace, jnp.bfloat16),
                pltpu.VMEM(trace, jnp.bfloat16),
                pltpu.VMEM((STEPS - 1, n // 2, *trace), jnp.bfloat16),
                pltpu.VMEM((STEPS - 1, n // 2, *trace), jnp.bfloat16),
                pltpu.VMEM((STEPS - 1, n // 2, *trace), jnp.bfloat16),
                pltpu.VMEM((STEPS - 1, n // 2, *trace), jnp.bfloat16),
                pltpu.VMEM((n, *trace), jnp.bfloat16),
                pltpu.VMEM((n, *trace), jnp.bfloat16),
                dma((6,)),
                dma((STEPS, n)),
                dma((STEPS, n)),
                dma,
                dma,
                dma,
                dma,
                dma,
                dma,
                dma((STEPS - 1, n // 2)),
                dma((STEPS - 1, n // 2)),
                dma((STEPS - 1, n // 2)),
                dma((STEPS - 1, n // 2)),
                dma((STEPS - 1, n // 2)),
                dma((n,)),
                dma((n,)),
            ],
            compiler_params=pltpu.CompilerParams(
                collective_id=0, has_side_effects=True
            ),
        )(up_source, down_source, source_layer.reshape(1, sources), u_factor, v_factor, block_rank)
        return pl.pallas_call(
            hand_over,
            out_shape=(
                jax.ShapeDtypeStruct(up_source.shape, jnp.bfloat16),
                jax.ShapeDtypeStruct(down_source.shape, jnp.bfloat16),
            ),
            in_specs=[anywhere, anywhere],
            out_specs=(anywhere, anywhere),
            scratch_shapes=[
                pltpu.VMEM(up_source.shape, jnp.bfloat16),
                pltpu.VMEM(down_source.shape, jnp.bfloat16),
                dma((2, 2)),
            ],
        )(*traces)

    in_specs = (
        P("gz", None, None, "xy"),
        P("gz", None, None, "xy"),
        P(),
        P("gz", "xy", None, None, None, None),
        P("gz", "xy", None, None, None, None),
        P("gz", "xy", None),
    )
    out_specs = (P("gz", None, None, "xy"), P("gz", None, None, "xy"))
    return jax.shard_map(
        on_device, mesh=mesh, in_specs=in_specs, out_specs=out_specs, check_vma=False
    )
```

```python
import functools

import jax
import jax.numpy as jnp
from jax import lax
from jax.experimental import pallas as pl
from jax.experimental.pallas import tpu as pltpu
from jax.sharding import PartitionSpec as P

STEPS = 3
MESH = pl.DeviceIdType.MESH


def kernel(
    layers, n, up_hbm, down_hbm, layer_hbm, u_hbm, v_hbm, rank_hbm, up_out, down_out,
    up_ref, down_ref, layer_ref, rank_ref, down_done,
    u_mem, v_mem, up_all, up_send, up_next, up_last, own_down, down_first, part, part_send,
    twin_part, twin_send, last_in, last_send,
    load_sem, up_ssem, up_rsem, next_ssem, next_rsem, last_ssem, last_rsem,
    first_ssem, first_rsem, part_ssem, part_rsem,
    relay_ssem, twin_ssem, twin_rsem, last_part_ssem, last_part_rsem,
):
    layer = lax.axis_index("gz")
    me = lax.axis_index("xy")
    has_above = layer < layers - 1
    has_below = layer > 0
    rows, width = up_send.shape[1:]
    sources = rows // 2
    max_rank = u_mem.shape[2]
    others = [lax.rem(me + k, n) for k in range(n)]
    core = lax.rem(me, 2)
    twin = me + 1 - 2 * core
    like = [lax.rem(me + 2 * k, n) for k in range(n // 2)]
    unlike = [lax.rem(twin + 2 * k, n) for k in range(n // 2)]
    chip = me // 2

    def remote(src, dst, ssem, rsem, to_layer, to_block):
        return pltpu.make_async_remote_copy(
            src_ref=src, dst_ref=dst, send_sem=ssem, recv_sem=rsem,
            device_id={"gz": to_layer, "xy": to_block}, device_id_type=MESH,
        )

    load_u = pltpu.make_async_copy(u_hbm.at[0, 0], u_mem, load_sem.at[0])
    load_v = pltpu.make_async_copy(v_hbm.at[0, 0], v_mem, load_sem.at[1])
    small = [
        pltpu.make_async_copy(src, dst, load_sem.at[2 + i])
        for i, (src, dst) in enumerate(
            [(layer_hbm, layer_ref), (up_hbm.at[0], up_ref), (down_hbm.at[0], down_ref), (rank_hbm, rank_ref)]
        )
    ]
    for load in small:
        load.start()

    barrier = pltpu.get_barrier_semaphore()

    def greet(to_layer, to_block):
        pl.semaphore_signal(
            barrier, inc=1, device_id={"gz": to_layer, "xy": to_block}, device_id_type=MESH
        )

    for k in range(1, n):
        greet(layer, others[k])

    @pl.when(has_above)
    def _():
        for k in range(n // 2):
            greet(layer + 1, like[k])

    @pl.when(has_below)
    def _():
        for k in range(n // 2):
            greet(layer - 1, like[k])

    load_v.start()
    load_u.start()
    for load in small:
        load.wait()
    square = (sources, sources)
    diagonal = lax.broadcasted_iota(jnp.int32, square, 0) == lax.broadcasted_iota(jnp.int32, square, 1)
    source_layer = jnp.sum(
        jnp.where(diagonal, jnp.broadcast_to(layer_ref[...], square), 0), axis=1, keepdims=True
    )
    source_layer = jnp.broadcast_to(jnp.concatenate([source_layer, source_layer], axis=0), (rows, width))
    up_own = jnp.where(
        layer >= source_layer, up_ref[...].reshape(rows, width).astype(jnp.float32), 0.0
    ).astype(jnp.bfloat16)
    down_own = jnp.where(
        layer <= source_layer, down_ref[...].reshape(rows, width).astype(jnp.float32), 0.0
    ).astype(jnp.bfloat16)
    up_all[0, me] = up_own
    own_down[...] = down_own

    @pl.when(jnp.logical_not(has_above))
    def _():
        up_next[...] = jnp.zeros_like(up_next)
        down_first[...] = jnp.zeros_like(down_first)
        part[0] = jnp.zeros_like(part[0])
        part[1] = jnp.zeros_like(part[1])

    peers = n - 1 + jnp.where(has_above, n // 2, 0) + jnp.where(has_below, n // 2, 0)
    pl.semaphore_wait(barrier, peers)

    def gather(k):
        return remote(
            up_all.at[0, me], up_all.at[0, me], up_ssem.at[0, k], up_rsem.at[0, me], layer, others[k]
        )

    def next_up():
        return remote(up_all.at[0, me], up_next, next_ssem, next_rsem, layer - 1, me)

    def first_down():
        return remote(own_down, down_first, first_ssem, first_rsem, layer - 1, me)

    def up_step(t, k):
        return remote(
            up_send.at[t], up_all.at[t + 1, me], up_ssem.at[t + 1, k], up_rsem.at[t + 1, me],
            layer + 1, like[k],
        )

    def relay(t, k):
        slot = up_all.at[t, like[k]]
        return remote(slot, slot, relay_ssem.at[t - 1, k], up_rsem.at[t, like[k]], layer, twin)

    def last_up():
        return remote(up_send.at[STEPS - 1], up_last, last_ssem, last_rsem, layer + 1, me)

    def part_step(t, k):
        return remote(
            part_send.at[t, k], part.at[t, chip], part_ssem.at[t, k], part_rsem.at[t, chip],
            layer - 1, like[k],
        )

    def twin_step(t, k):
        place = unlike[k] // 2
        return remote(
            twin_send.at[t, k], twin_part.at[t, place], twin_ssem.at[t, k], twin_rsem.at[t, place],
            layer, twin,
        )

    def last_part(k):
        return remote(
            last_send.at[k], last_in.at[me], last_part_ssem.at[k], last_part_rsem.at[me],
            layer, others[k],
        )

    def arrived(ref, rsem):
        remote(ref, ref, next_ssem, rsem, layer, me).wait_recv()

    far_first = [*range(2, n), 1]
    for k in far_first:
        gather(k).start()

    @pl.when(has_below)
    def _():
        first_down().start()
        next_up().start()

    rank_index = lax.broadcasted_iota(jnp.int32, (sources, max_rank), 1)

    def coefficients(trace, factor, block):
        product = lax.dot_general(
            trace, factor.reshape(2 * max_rank, width), (((1,), (1,)), ((), ())),
            preferred_element_type=jnp.float32,
        )
        keep = rank_index < (max_rank // 4) * rank_ref[0, 0, block]
        real = product[:sources, :max_rank] - product[sources:, max_rank:]
        imag = product[:sources, max_rank:] + product[sources:, :max_rank]
        real = jnp.where(keep, real, 0.0)
        imag = jnp.where(keep, imag, 0.0)
        return jnp.concatenate(
            [jnp.concatenate([real, -imag], axis=1), jnp.concatenate([imag, real], axis=1)], axis=0
        ).astype(jnp.bfloat16)

    def expand(coef, factor):
        return jnp.dot(
            coef, factor.reshape(2 * max_rank, width), preferred_element_type=jnp.float32
        )

    load_v.wait()
    load_u.wait()

    def wait_blocks(t, blocks):
        for block in blocks:
            arrived(up_all.at[t, block], up_rsem.at[t, block])

    for t in range(STEPS):
        last = t == STEPS - 1
        held = 0 if t == 0 else jnp.where(has_below, t, 0)

        def rise(block):
            return expand(coefficients(up_all[held, block], v_mem[block], block), u_mem[block])

        def piece(block):
            return expand(coefficients(down, u_mem[block], block), v_mem[block])

        if t > 0:

            @pl.when(has_below)
            def _():
                for k in reversed(range(n // 2)):
                    wait_blocks(t, [like[k]])
                    relay(t, k).start()

        @pl.when(has_above)
        def _():
            if t == 0:
                arrived(down_first, first_rsem)
            else:
                for k in range(n // 2):
                    place = like[k] // 2
                    arrived(part.at[t - 1, place], part_rsem.at[t - 1, place])

        down = down_first[...]
        if t > 0:
            total = down.astype(jnp.float32)
            for k in range(n // 2):
                total = total + part[t - 1, like[k] // 2].astype(jnp.float32)
            down = total.astype(jnp.bfloat16)

        if last:
            for k in far_first:
                last_send[k] = piece(others[k]).astype(jnp.bfloat16)
                last_part(k).start()
        else:
            for k in range(n // 2):
                twin_send[t, k] = piece(unlike[k]).astype(jnp.bfloat16)
                twin_step(t, k).start()

        if t == 0:
            wait_blocks(0, like[1:])
        total = sum([rise(block) for block in like])
        if t == 0:
            wait_blocks(0, unlike)

            @pl.when(has_above)
            def _():
                arrived(up_next, next_rsem)

        else:

            @pl.when(has_below)
            def _():
                wait_blocks(t, unlike)

        total = total + sum([rise(block) for block in unlike])
        up_send[t] = (up_next[...].astype(jnp.float32) + total).astype(jnp.bfloat16)

        @pl.when(has_above)
        def _():
            if last:
                last_up().start()
            else:
                for k in reversed(range(n // 2)):
                    up_step(t, k).start()

        if last:
            own_part = piece(me)
        else:
            pieces = [piece(block) for block in like]
            for k in range(n // 2):
                place = like[k] // 2
                arrived(twin_part.at[t, place], twin_rsem.at[t, place])
                part_send[t, k] = (pieces[k] + twin_part[t, place].astype(jnp.float32)).astype(
                    jnp.bfloat16
                )

            @pl.when(has_below)
            def _():
                for k in reversed(range(n // 2)):
                    part_step(t, k).start()

    total = own_down[...].astype(jnp.float32) + own_part
    for k in range(1, n):
        arrived(last_in.at[others[k]], last_part_rsem.at[others[k]])
        total = total + last_in[others[k]].astype(jnp.float32)
    down_done[...] = total.astype(jnp.bfloat16).reshape(2, sources, width)
    put_down = pltpu.make_async_copy(down_done, down_out.at[0], load_sem.at[0])
    put_down.start()

    @pl.when(has_below)
    def _():
        arrived(up_last, last_rsem)
        up_ref[...] = up_last[...].reshape(2, sources, width)

    @pl.when(jnp.logical_not(has_below))
    def _():
        up_ref[...] = up_all[0, me].reshape(2, sources, width)

    put_up = pltpu.make_async_copy(up_ref, up_out.at[0], load_sem.at[1])
    put_up.start()

    for k in range(1, n):
        gather(k).wait_send()
        last_part(k).wait_send()
    for t in range(STEPS - 1):
        for k in range(n // 2):
            twin_step(t, k).wait_send()

    @pl.when(has_below)
    def _():
        first_down().wait_send()
        next_up().wait_send()
        for t in range(STEPS - 1):
            for k in range(n // 2):
                part_step(t, k).wait_send()
                relay(t + 1, k).wait_send()

    @pl.when(has_above)
    def _():
        for t in range(STEPS - 1):
            for k in range(n // 2):
                up_step(t, k).wait_send()
        last_up().wait_send()

    put_down.wait()
    put_up.wait()


def hand_over(up_ref, down_ref, up_out, down_out, up_mem, down_mem, sems):
    pairs = [(up_ref, up_mem, up_out), (down_ref, down_mem, down_out)]
    loads = [pltpu.make_async_copy(src, mem, sems.at[0, i]) for i, (src, mem, _) in enumerate(pairs)]
    stores = [pltpu.make_async_copy(mem, dst, sems.at[1, i]) for i, (_, mem, dst) in enumerate(pairs)]
    for load in loads:
        load.start()
    for load, store in zip(loads, stores):
        load.wait()
        store.start()
    for store in stores:
        store.wait()


def solution(mesh):
    layers, n = mesh.shape["gz"], mesh.shape["xy"]

    def on_device(up_source, down_source, source_layer, u_factor, v_factor, block_rank):
        _, _, sources, width = up_source.shape
        rows = 2 * sources
        trace = (rows, width)
        anywhere = pl.BlockSpec(memory_space=pl.ANY)
        hbm = pl.BlockSpec(memory_space=pltpu.HBM)
        dma = pltpu.SemaphoreType.DMA
        traces = pl.pallas_call(
            functools.partial(kernel, layers, n),
            out_shape=(
                jax.ShapeDtypeStruct(up_source.shape, jnp.bfloat16),
                jax.ShapeDtypeStruct(down_source.shape, jnp.bfloat16),
            ),
            in_specs=[hbm] * 6,
            out_specs=(anywhere, anywhere),
            scratch_shapes=[
                pltpu.VMEM((2, sources, width), jnp.bfloat16),
                pltpu.VMEM((2, sources, width), jnp.bfloat16),
                pltpu.VMEM((1, sources), jnp.int32),
                pltpu.SMEM(block_rank.shape, jnp.int32),
                pltpu.VMEM((2, sources, width), jnp.bfloat16),
                pltpu.VMEM(u_factor.shape[2:], jnp.bfloat16),
                pltpu.VMEM(v_factor.shape[2:], jnp.bfloat16),
                pltpu.VMEM((STEPS, n, *trace), jnp.bfloat16),
                pltpu.VMEM((STEPS, *trace), jnp.bfloat16),
                pltpu.VMEM(trace, jnp.bfloat16),
                pltpu.VMEM(trace, jnp.bfloat16),
                pltpu.VMEM(trace, jnp.bfloat16),
                pltpu.VMEM(trace, jnp.bfloat16),
                pltpu.VMEM((STEPS - 1, n // 2, *trace), jnp.bfloat16),
                pltpu.VMEM((STEPS - 1, n // 2, *trace), jnp.bfloat16),
                pltpu.VMEM((STEPS - 1, n // 2, *trace), jnp.bfloat16),
                pltpu.VMEM((STEPS - 1, n // 2, *trace), jnp.bfloat16),
                pltpu.VMEM((n, *trace), jnp.bfloat16),
                pltpu.VMEM((n, *trace), jnp.bfloat16),
                dma((6,)),
                dma((STEPS, n)),
                dma((STEPS, n)),
                dma,
                dma,
                dma,
                dma,
                dma,
                dma,
                dma((STEPS - 1, n // 2)),
                dma((STEPS - 1, n // 2)),
                dma((STEPS - 1, n // 2)),
                dma((STEPS - 1, n // 2)),
                dma((STEPS - 1, n // 2)),
                dma((n,)),
                dma((n,)),
            ],
            compiler_params=pltpu.CompilerParams(
                collective_id=0, has_side_effects=True
            ),
        )(up_source, down_source, source_layer.reshape(1, sources), u_factor, v_factor, block_rank)
        return pl.pallas_call(
            hand_over,
            out_shape=(
                jax.ShapeDtypeStruct(up_source.shape, jnp.bfloat16),
                jax.ShapeDtypeStruct(down_source.shape, jnp.bfloat16),
            ),
            in_specs=[anywhere, anywhere],
            out_specs=(anywhere, anywhere),
            scratch_shapes=[
                pltpu.VMEM(up_source.shape, jnp.bfloat16),
                pltpu.VMEM(down_source.shape, jnp.bfloat16),
                dma((2, 2)),
            ],
        )(*traces)

    in_specs = (
        P("gz", None, None, "xy"),
        P("gz", None, None, "xy"),
        P(),
        P("gz", "xy", None, None, None, None),
        P("gz", "xy", None, None, None, None),
        P("gz", "xy", None),
    )
    out_specs = (P("gz", None, None, "xy"), P("gz", None, None, "xy"))
    return jax.shard_map(
        on_device, mesh=mesh, in_specs=in_specs, out_specs=out_specs, check_vma=False
    )
```
